512 devices in a mesh: row: 32 (over x, y, core), col: 16 (over z).
Axes of the slice: x: 4, y: 4, z: 16, core: 2. Of those that a mesh axis runs over, the one named last changes fastest.
Arguments:
- mixture_fractions: float32 [54, 256, 2048], P(None, 'row', 'col'), may hold values from -6 to 6
- spreading_coefficient: float32 [256, 2048], P('row', 'col'), may hold values from 0.02 to 0.12
- flow_speed_vector: float32 [2, 256, 2048], P(None, 'row', 'col'), may hold values from -0.15 to 0.15
- thermal_state: float32 [256, 2048], P('row', 'col'), may hold values from -6 to 6
- chemistry_active_indicator: int32 [256, 2048], P('row', 'col'), may hold values from 0 to 1, as said below
- entry_level_matrix: bfloat16 [256, 55], replicated, may hold values from -0.875 to 0.875
- entry_level_offset: float32 [256], replicated, may hold values from -3 to 3
- hidden_level_matrix: bfloat16 [256, 256], replicated, may hold values from -0.375 to 0.375
- hidden_level_offset: float32 [256], replicated, may hold values from -3 to 3
- final_level_matrix: bfloat16 [54, 256], replicated, may hold values from -0.375 to 0.375
- final_level_offset: float32 [54], replicated, may hold values from -3 to 3
Outputs:
- species_next: float32 [54, 256, 2048], P(None, 'row', 'col')
The draws below stay inside these ranges and needn't reach their ends.
Inputs may be any that keep to these rules, and one draw needn't show every extreme that they name: `chemistry_active_indicator`: split the grid into tiles of 8 x 128 cells and bands of 8 rows. Every tile holds at most 384 flagged cells, and in every band some tile holds exactly 384; every band holds exactly 2048 flagged cells.
All inputs are finite; a program needn't handle non-finite values.
Results may differ from the reference program's by a relative error of at most 0.0003.
Values sent between devices are 32-bit elements; how exact they have to be, the bound alone decides.
No kernel may reach another device: no remote copies, remote signals or barrier semaphores. Data moves between devices by JAX's collectives and lax.ppermute only.
A program may use at most 64 MiB of HBM per device.

```python
import math
import jax
import jax.numpy as jnp
from jax import lax

CHEMICAL_KINDS = 54
HID = 256
SUBSTEPS = 8
TRANSPORT_STEPS = 3
CY = 8
CX = 128
MESH_HEIGHT = 256
MESH_WIDTH = 2048
ROW_SHARE = 128
N_ROW = 32
N_COL = 16


def draw_chemistry_active_indicator(key, part):
    first_key, second_key, third_key = jax.random.split(key, 3)
    share_cells = CY * CX // 8
    cell_capacity = 3 * share_cells
    cell_total = CY * CX
    remainder = N_COL * share_cells - cell_capacity
    weights = jax.random.randint(first_key, (N_ROW, N_COL), 2, 6)
    busiest = jax.random.randint(second_key, (N_ROW,), 0, N_COL)
    holds_most_work = jnp.arange(N_COL)[None, :] == busiest[:, None]
    weights = jnp.where(holds_most_work, 0, weights)
    lowest_share = remainder * weights // jnp.sum(weights, axis=1, keepdims=True)
    leftover_cells = remainder - jnp.sum(lowest_share, axis=1, keepdims=True)
    drawn_position = jnp.cumsum(jnp.where(holds_most_work, 0, 1), axis=1) - 1
    extra_cell = jnp.where(jnp.logical_and(jnp.logical_not(holds_most_work), drawn_position < leftover_cells), 1, 0)
    flagged_counts = jnp.where(holds_most_work, cell_capacity, lowest_share + extra_cell).reshape(-1, 1)
    subkeys = jax.random.split(third_key, N_ROW * N_COL)
    orders = jax.vmap(lambda single: jax.random.permutation(single, cell_total))(subkeys)
    active = (orders < flagged_counts).astype(jnp.int32)
    active = active.reshape(N_ROW, N_COL, CY, CX).transpose(0, 2, 1, 3)
    return active.reshape(CY * N_ROW, CX * N_COL)


def level_of(stream_key, shape, pieces, low, high):
    level = 1.0
    for dim, parts in pieces:
        steps = jax.random.uniform(jax.random.fold_in(jax.random.fold_in(stream_key, 6), dim), (parts,), jnp.float32, low / len(pieces), high / len(pieces))
        level = level * jnp.repeat(jnp.exp(steps), shape[dim] // parts).reshape((-1,) + (1,) * (len(shape) - 1 - dim))
    return level


def noise(rng, shape, width, limit, cuts=(), kind=jnp.bfloat16):
    values = width * jax.random.normal(rng, shape, jnp.float32)
    if cuts:
        values = values * level_of(rng, shape, cuts, -0.22, 0.18)
    return jnp.clip(values, -limit, limit).astype(kind)


def setup_inputs(seed: int = 0) -> dict:
    key_list = jax.random.split(jax.random.key(seed), 12)
    mixture_fractions = noise(key_list[0], (CHEMICAL_KINDS, MESH_HEIGHT, MESH_WIDTH), 1.0, 6.0, ((1, 32), (2, 16)), jnp.float32)
    spreading_coefficient = jnp.clip(jnp.exp(math.log(0.12) - 1.7917595 * jax.random.uniform(key_list[1], (MESH_HEIGHT, MESH_WIDTH), jnp.float32) ** level_of(key_list[1], (MESH_HEIGHT, MESH_WIDTH), ((0, 32), (1, 16)), -0.2, 0.2)), 0.02, 0.12)
    flow_speed_vector = jnp.clip(jax.random.uniform(key_list[2], (2, MESH_HEIGHT, MESH_WIDTH), jnp.float32, -0.15, 0.15) * level_of(key_list[2], (2, MESH_HEIGHT, MESH_WIDTH), ((1, 32), (2, 16)), -0.4, 0.0), -0.15, 0.15)
    thermal_state = noise(key_list[3], (MESH_HEIGHT, MESH_WIDTH), 1.0, 6.0, ((0, 32), (1, 16)), jnp.float32)
    chemistry_active_indicator = draw_chemistry_active_indicator(jax.random.fold_in(key_list[11], 71), 0)
    entry_level_matrix = noise(key_list[5], (HID, CHEMICAL_KINDS + 1), (CHEMICAL_KINDS + 1) ** -0.5, 0.875)
    entry_level_offset = noise(key_list[6], (HID,), 0.5, 3.0, (), jnp.float32)
    hidden_level_matrix = noise(key_list[7], (HID, HID), HID ** -0.5, 0.375)
    hidden_level_offset = noise(key_list[8], (HID,), 0.5, 3.0, (), jnp.float32)
    final_level_matrix = noise(key_list[9], (CHEMICAL_KINDS, HID), HID ** -0.5, 0.375)
    final_level_offset = noise(key_list[10], (CHEMICAL_KINDS,), 0.5, 3.0, (), jnp.float32)
    return {"mixture_fractions": mixture_fractions, "spreading_coefficient": spreading_coefficient, "flow_speed_vector": flow_speed_vector, "thermal_state": thermal_state, "chemistry_active_indicator": chemistry_active_indicator, "entry_level_matrix": entry_level_matrix, "entry_level_offset": entry_level_offset, "hidden_level_matrix": hidden_level_matrix, "hidden_level_offset": hidden_level_offset, "final_level_matrix": final_level_matrix, "final_level_offset": final_level_offset}


time_step = 1.0
chem_step = 0.0625


def advance(padded, pad_diff, speed_cols, speed_rows):
    left_vals = padded[..., 1:-1, :-1]
    right_vals = padded[..., 1:-1, 1:]
    face_diff = 0.5 * (pad_diff[1:-1, :-1] + pad_diff[1:-1, 1:])
    face_speed = 0.5 * (speed_cols[1:-1, :-1] + speed_cols[1:-1, 1:])
    flux_cols = face_diff * (right_vals - left_vals) - (jnp.maximum(face_speed, 0.0) * left_vals + jnp.minimum(face_speed, 0.0) * right_vals)
    lower_vals = padded[..., :-1, 1:-1]
    upper_vals = padded[..., 1:, 1:-1]
    face_diff = 0.5 * (pad_diff[:-1, 1:-1] + pad_diff[1:, 1:-1])
    face_speed = 0.5 * (speed_rows[:-1, 1:-1] + speed_rows[1:, 1:-1])
    flux_rows = face_diff * (upper_vals - lower_vals) - (jnp.maximum(face_speed, 0.0) * lower_vals + jnp.minimum(face_speed, 0.0) * upper_vals)
    change = flux_cols[..., 1:] - flux_cols[..., :-1] + flux_rows[..., 1:, :] - flux_rows[..., :-1, :]
    return padded[..., 1:-1, 1:-1] + time_step * change


def network(inputs, entry_level_matrix, entry_level_offset, hidden_level_matrix, hidden_level_offset, final_level_matrix, final_level_offset):
    hidden = jnp.tanh(jnp.dot(entry_level_matrix, inputs, preferred_element_type=jnp.float32) + entry_level_offset[:, None]).astype(jnp.bfloat16)
    hidden = jnp.tanh(jnp.dot(hidden_level_matrix, hidden, preferred_element_type=jnp.float32) + hidden_level_offset[:, None]).astype(jnp.bfloat16)
    return jnp.dot(final_level_matrix, hidden, preferred_element_type=jnp.float32) + final_level_offset[:, None]


def integrate(state, heat, entry_level_matrix, entry_level_offset, hidden_level_matrix, hidden_level_offset, final_level_matrix, final_level_offset):
    total = jnp.zeros(state.shape, jnp.float32)
    for index in range(SUBSTEPS):
        inputs = jnp.concatenate([state + chem_step * total, heat[None]], 0).astype(jnp.bfloat16)
        total = total + network(inputs, entry_level_matrix, entry_level_offset, hidden_level_matrix, hidden_level_offset, final_level_matrix, final_level_offset)
    return chem_step * total


def reference(mixture_fractions, spreading_coefficient, flow_speed_vector, thermal_state, chemistry_active_indicator, entry_level_matrix, entry_level_offset, hidden_level_matrix, hidden_level_offset, final_level_matrix, final_level_offset):
    pad_diff = jnp.pad(spreading_coefficient, 1)
    pad_speed = jnp.pad(flow_speed_vector, ((0, 0), (1, 1), (1, 1)))
    carried_quantity = mixture_fractions
    for section in range(TRANSPORT_STEPS):
        carried_quantity = lax.map(lambda field: advance(jnp.pad(field, 1), pad_diff, pad_speed[0], pad_speed[1]), carried_quantity)
    predictor_vector = jnp.concatenate([carried_quantity, thermal_state[None]], 0).reshape(CHEMICAL_KINDS + 1, MESH_HEIGHT * MESH_WIDTH)
    cell_total = MESH_HEIGHT * MESH_WIDTH
    chosen = jnp.nonzero(chemistry_active_indicator.reshape(-1), size=cell_total // 8, fill_value=cell_total)[0].astype(jnp.int32)
    blocks = chosen.reshape(-1, ROW_SHARE)

    def per_block(cells_here):
        inputs = jnp.take(predictor_vector, cells_here, axis=1, mode="fill", fill_value=0)
        return integrate(inputs[:CHEMICAL_KINDS], inputs[CHEMICAL_KINDS], entry_level_matrix, entry_level_offset, hidden_level_matrix, hidden_level_offset, final_level_matrix, final_level_offset)

    rates = lax.map(per_block, blocks)
    rates = jnp.transpose(rates, (1, 0, 2)).reshape(CHEMICAL_KINDS, -1)
    increments = jnp.zeros((CHEMICAL_KINDS, cell_total + 1), jnp.float32).at[:, chosen].add(rates)[:, :cell_total]
    return (carried_quantity.reshape(CHEMICAL_KINDS, cell_total) + increments).reshape(CHEMICAL_KINDS, MESH_HEIGHT, MESH_WIDTH)
```

```python
import functools

import jax
import jax.numpy as jnp
from jax import lax
from jax.experimental import pallas as pl
from jax.experimental.pallas import tpu as pltpu
from jax.sharding import PartitionSpec as P

SUBSTEPS = 8
STEPS = 3
KINDS = 54
HID = 256
ROWS = 8
LANES = 128
CAP = 384
CHUNK = 128
CHANNELS = 64
DIFF, SPEED_C, SPEED_R, INSIDE = 54, 55, 56, 57
WIDE = 10
chem_step = 0.0625
f32 = jnp.float32
bf16 = jnp.bfloat16


def iota(shape, axis):
    return lax.broadcasted_iota(jnp.int32, shape, axis)


def planes_kernel(y_ref, d_ref, v_ref, all_ref, top_ref, bottom_ref):
    for r in range(ROWS):
        refs = [all_ref.at[r]]
        if r < STEPS:
            refs.append(top_ref.at[r])
        if r >= ROWS - STEPS:
            refs.append(bottom_ref.at[r - ROWS + STEPS])
        species = y_ref[:, r, :]
        for ref in refs:
            ref[0:KINDS, :] = species
            ref[DIFF : DIFF + 1, :] = d_ref[r : r + 1, :]
            ref[SPEED_C : SPEED_C + 1, :] = v_ref[0, r : r + 1, :]
            ref[SPEED_R : SPEED_R + 1, :] = v_ref[1, r : r + 1, :]
            ref[INSIDE:CHANNELS, :] = jnp.ones((CHANNELS - INSIDE, LANES), f32)


def strip_kernel(all_ref, low_ref, high_ref, strip_ref):
    lane = iota((CHANNELS, LANES), 1)
    total = jnp.zeros((CHANNELS, LANES), f32)
    for j in range(ROWS + 4):
        row = j - 2
        if row < 0:
            plane = low_ref[STEPS + row]
        elif row < ROWS:
            plane = all_ref[row]
        else:
            plane = high_ref[row - ROWS]
        at = WIDE * j
        first = pltpu.roll(plane, (at + 3) % LANES, 1)
        second = pltpu.roll(plane, (at + 7) % LANES, 1)
        total = jnp.where((lane >= at) & (lane < at + 5), first, total)
        total = jnp.where((lane >= at + 5) & (lane < at + WIDE), second, total)
    strip_ref[...] = total


def prepare_kernel(act_ref, w1_ref, w2_ref, w3_ref, b3_ref, pick_ref, w1t_ref, w2t_ref, mix_ref, w3t_ref, bias_ref):
    act = act_ref[...].astype(f32)
    before = (iota((LANES, LANES), 0) < iota((LANES, LANES), 1)).astype(f32).astype(bf16)
    inner = jnp.dot(act.astype(bf16), before, preferred_element_type=f32)
    counts = jnp.broadcast_to(jnp.sum(act, axis=1, keepdims=True), (ROWS, LANES))
    row = iota((ROWS, LANES), 0)
    outer = jnp.zeros((ROWS, LANES), f32)
    for k in range(ROWS - 1):
        outer = outer + jnp.where(row > k, jnp.broadcast_to(counts[k : k + 1, :], (ROWS, LANES)), 0.0)
    slot = jnp.where(act > 0.0, inner + outer, -1.0).astype(jnp.int32)
    slots = iota((CAP, LANES), 0)
    for r in range(ROWS):
        hit = slots == jnp.broadcast_to(slot[r : r + 1, :], (CAP, LANES))
        pick_ref[:, r * LANES : (r + 1) * LANES] = jnp.where(hit, 1.0, 0.0).astype(bf16)
    w1t = w1_ref[...].astype(f32).T
    w1t_ref[...] = jnp.zeros((2 * CHANNELS, HID), bf16)
    for k in range(2):
        w1t_ref[k * CHANNELS : k * CHANNELS + KINDS + 1, :] = w1t.astype(bf16)
    w2t_ref[...] = w2_ref[...].astype(f32).T.astype(bf16)
    w3t = w3_ref[...].astype(f32).T
    w3t_ref[...] = w3t.astype(bf16)
    part = w1t[0:KINDS, :]
    mix = jnp.dot(w3t.astype(bf16), part.astype(bf16), preferred_element_type=f32)
    mix_ref[...] = (chem_step * mix).astype(bf16)
    bias_ref[...] = chem_step * jnp.sum(part * b3_ref[...], axis=0, keepdims=True)


def face(d_low, d_high, u_low, u_high):
    d = 0.5 * (d_low + d_high)
    u = 0.5 * (u_low + u_high)
    return d - jnp.minimum(u, 0.0), d + jnp.maximum(u, 0.0)


def main_kernel(
    all_ref, low_ref, high_ref, own_ref, left_ref, right_ref, heat_ref,
    pick_ref, w1t_ref, w2t_ref, mix_ref, w3t_ref, bias_ref, b1_ref, b2_ref, b3_ref,
    out_ref, base_ref, coef_ref, one_ref, two_ref, feat_ref, pre_ref, sum_ref,
):
    lane = iota((CHANNELS, LANES), 1)
    place = lane % WIDE
    strip = jnp.where(place < 3, left_ref[...], jnp.where(place < 7, own_ref[...], right_ref[...]))
    lane1 = iota((1, LANES), 1)
    ds, us, vs, inside = (strip[k : k + 1, :] for k in (DIFF, SPEED_C, SPEED_R, INSIDE))
    inside = jnp.where(lane1 < WIDE * (ROWS + 4), inside, 0.0)
    ahead, behind = LANES - 1, 1
    a_r, b_r = face(ds, pltpu.roll(ds, ahead, 1), us, pltpu.roll(us, ahead, 1))
    a_l, b_l = pltpu.roll(a_r, behind, 1), pltpu.roll(b_r, behind, 1)
    a_u, b_u = face(ds, pltpu.roll(ds, LANES - WIDE, 1), vs, pltpu.roll(vs, LANES - WIDE, 1))
    a_d, b_d = pltpu.roll(a_u, WIDE, 1), pltpu.roll(b_u, WIDE, 1)
    strip_coef = [
        jnp.broadcast_to(inside * c, (56, LANES)) for c in (1.0 - b_r - a_l - b_u - a_d, a_r, b_l, a_u, b_d)
    ]
    for k in range(4):
        for i in range(STEPS):
            base_ref[k, 8 + i : 9 + i, :] = low_ref[i, DIFF + k : DIFF + k + 1, :]
            base_ref[k, 19 + i : 20 + i, :] = high_ref[i, DIFF + k : DIFF + k + 1, :]
        base_ref[k, 0:8, :] = jnp.zeros((8, LANES), f32)
        base_ref[k, 22:32, :] = jnp.zeros((10, LANES), f32)
        for r in range(ROWS):
            base_ref[k, 11 + r : 12 + r, :] = all_ref[r, DIFF + k : DIFF + k + 1, :]
    here, up, down = (lambda k: base_ref[k, 8:24, :]), (lambda k: base_ref[k, 9:25, :]), (lambda k: base_ref[k, 7:23, :])
    lane16, row16 = iota((16, LANES), 1), iota((16, LANES), 0)

    def column(values, c):
        hit = lane16 == WIDE * (row16 - 1) + c
        return jnp.sum(jnp.where(hit, jnp.broadcast_to(values, (16, LANES)), 0.0), axis=1, keepdims=True)

    d, u, v, ins = here(0), here(1), here(2), here(3)
    after = lambda x, s: jnp.where(lane16 == LANES - 1, column(s, 7), pltpu.roll(x, ahead, 1))
    prior = lambda x, s: jnp.where(lane16 == 0, column(s, 2), pltpu.roll(x, behind, 1))
    a_r, b_r = face(d, after(d, ds), u, after(u, us))
    a_l, b_l = face(prior(d, ds), d, prior(u, us), u)
    a_u, b_u = face(d, up(0), v, up(2))
    a_d, b_d = face(down(0), d, down(2), v)
    for k, c in enumerate((1.0 - b_r - a_l - b_u - a_d, a_r, b_l, a_u, b_d)):
        coef_ref[k] = ins * c

    def load(step, i):
        if step == 0:
            if i < STEPS:
                return low_ref[i, 0:56, :]
            if i < STEPS + ROWS:
                return all_ref[i - STEPS, 0:56, :]
            return high_ref[i - STEPS - ROWS, 0:56, :]
        return (one_ref if step % 2 else two_ref)[i]

    edge = iota((56, LANES), 1)
    strip = strip[0:56, :]
    for step in range(STEPS):
        target = two_ref if step % 2 else one_ref
        for i in range(1 + step, 13 - step):
            mine = load(step, i)
            at = WIDE * (i - 1)
            after_v = jnp.where(edge == LANES - 1, pltpu.roll(strip, (2 * LANES - 8 - at) % LANES, 1), pltpu.roll(mine, ahead, 1))
            prior_v = jnp.where(edge == 0, pltpu.roll(strip, (2 * LANES - 2 - at) % LANES, 1), pltpu.roll(mine, behind, 1))
            c = [jnp.broadcast_to(coef_ref[k, i : i + 1, :], (56, LANES)) for k in range(5)]
            target[i] = (
                c[0] * mine + c[1] * after_v + c[2] * prior_v + c[3] * load(step, i + 1) + c[4] * load(step, i - 1)
            )
        if step < STEPS - 1:
            strip = (
                strip_coef[0] * strip
                + strip_coef[1] * pltpu.roll(strip, ahead, 1)
                + strip_coef[2] * pltpu.roll(strip, behind, 1)
                + strip_coef[3] * pltpu.roll(strip, LANES - WIDE, 1)
                + strip_coef[4] * pltpu.roll(strip, WIDE, 1)
            )
    moved = one_ref if STEPS % 2 else two_ref

    sub = iota((56, LANES), 0)
    for r in range(ROWS):
        block = jnp.where(sub < KINDS, moved[r + STEPS], 0.0)
        block = jnp.where(sub == KINDS, jnp.broadcast_to(heat_ref[r : r + 1, :], (56, LANES)), block)
        block = jnp.concatenate([block, jnp.zeros((8, LANES), f32)], 0)
        coarse = block.astype(bf16)
        fine = jnp.where(iota((CHANNELS, LANES), 0) < KINDS, block - coarse.astype(f32), 0.0).astype(bf16)
        feat_ref[0:CHANNELS, r * LANES : (r + 1) * LANES] = coarse
        feat_ref[CHANNELS:, r * LANES : (r + 1) * LANES] = fine
    slots = lax.dot_general(pick_ref[...], feat_ref[...], (((1,), (1,)), ((), ())), preferred_element_type=f32)
    for k in range(CAP // CHUNK):
        s = slice(k * CHUNK, (k + 1) * CHUNK)
        pre_ref[s, :] = jnp.dot(slots[s, :].astype(bf16), w1t_ref[...], preferred_element_type=f32) + b1_ref[...]
    for index in range(SUBSTEPS):
        for k in range(CAP // CHUNK):
            s = slice(k * CHUNK, (k + 1) * CHUNK)
            first = jnp.tanh(pre_ref[s, :]).astype(bf16)
            second = jnp.dot(first, w2t_ref[...], preferred_element_type=f32) + b2_ref[...]
            second = jnp.tanh(second).astype(bf16)
            wide = second.astype(f32)
            sum_ref[s, :] = wide if index == 0 else sum_ref[s, :] + wide
            if index < SUBSTEPS - 1:
                pre_ref[s, :] += jnp.dot(second, mix_ref[...], preferred_element_type=f32) + bias_ref[...]
    total = sum_ref[...]
    high = total.astype(bf16)
    low = (total - high.astype(f32)).astype(bf16)
    rate = jnp.dot(high, w3t_ref[...], preferred_element_type=f32) + jnp.dot(low, w3t_ref[...], preferred_element_type=f32)
    rate = chem_step * (rate + SUBSTEPS * b3_ref[...])
    rate = jnp.concatenate([rate, jnp.zeros((CAP, LANES - KINDS), f32)], 1).T[0:56, :]
    high = rate.astype(bf16)
    low = (rate - high.astype(f32)).astype(bf16)
    for r in range(ROWS):
        block = pick_ref[:, r * LANES : (r + 1) * LANES]
        gain = jnp.dot(high, block, preferred_element_type=f32) + jnp.dot(low, block, preferred_element_type=f32)
        out_ref[:, r, :] = (moved[r + STEPS] + gain)[0:KINDS, :]


def vmem(count):
    return [pl.BlockSpec(memory_space=pltpu.VMEM)] * count


def call(kernel, shapes, operands, name, scratch=(), cost=None):
    return pl.pallas_call(
        kernel,
        out_shape=[jax.ShapeDtypeStruct(s, t) for s, t in shapes],
        in_specs=vmem(len(operands)),
        out_specs=vmem(len(shapes)),
        scratch_shapes=[pltpu.VMEM(s, t) for s, t in scratch],
        compiler_params=pltpu.CompilerParams(vmem_limit_bytes=16 << 20),
        cost_estimate=cost,
        name=name,
    )(*operands)


def shift(low_sends, high_sends, axis):
    devices = lax.axis_size(axis)
    up = [(i, i + 1) for i in range(devices - 1)]
    return lax.ppermute(low_sends, axis, up), lax.ppermute(high_sends, axis, [(b, a) for a, b in up])


def shards(y, d, v, heat, active, w1, b1, w2, b2, w3, b3):
    plane = (CHANNELS, LANES)
    every, top, bottom = call(
        planes_kernel, [((ROWS,) + plane, f32), ((STEPS,) + plane, f32), ((STEPS,) + plane, f32)], (y, d, v), "planes"
    )
    low, high = shift(bottom, top, "row")
    (strip,) = call(strip_kernel, [(plane, f32)], (every, low, high), "strip")
    left, right = shift(strip, strip, "col")
    picks = call(
        prepare_kernel,
        [((CAP, ROWS * LANES), bf16), ((2 * CHANNELS, HID), bf16), ((HID, HID), bf16), ((HID, HID), bf16), ((HID, KINDS), bf16), ((1, HID), f32)],
        (active, w1, w2, w3, b3[:, None]),
        "prepare",
        cost=pl.CostEstimate(flops=20_000_000, bytes_accessed=2_000_000, transcendentals=0),
    )
    (out,) = call(
        main_kernel,
        [((KINDS, ROWS, LANES), f32)],
        (every, low, high, strip, left, right, heat, *picks, b1[None], b2[None], b3[None]),
        "main",
        scratch=[
            ((4, 32, LANES), f32), ((5, 16, LANES), f32), ((14, 56, LANES), f32), ((14, 56, LANES), f32),
            ((2 * CHANNELS, ROWS * LANES), bf16), ((CAP, HID), f32), ((CAP, HID), f32),
        ],
    )
    return out


def solution(mesh):
    tile, rest = P("row", "col"), P()
    stack = P(None, "row", "col")
    in_specs = (stack, tile, stack, tile, tile, rest, rest, rest, rest, rest, rest)
    return jax.shard_map(shards, mesh=mesh, in_specs=in_specs, out_specs=stack, check_vma=False)
```

```python
import jax
import jax.numpy as jnp
from jax import lax
from jax.experimental import pallas as pl
from jax.experimental.pallas import tpu as pltpu
from jax.sharding import PartitionSpec as P

SUBSTEPS = 8
STEPS = 3
KINDS = 54
HID = 256
ROWS = 8
LANES = 128
CAP = 384
CHUNK = 128
CHANNELS = 64
DIFF, SPEED_C, SPEED_R, INSIDE = 54, 55, 56, 57
WIDE = 9
COST_PREPARE = 20_000_000
COST_MOVE = 20_000_000
chem_step = 0.0625
f32 = jnp.float32
bf16 = jnp.bfloat16


def iota(shape, axis):
    return lax.broadcasted_iota(jnp.int32, shape, axis)


def planes_kernel(y_hbm, d_hbm, v_hbm, all_ref, near_ref, far_ref, y_ref, d_ref, v_ref, sems):
    copies = [
        pltpu.make_async_copy(source, target, sems.at[k])
        for k, (source, target) in enumerate(((y_hbm, y_ref), (d_hbm, d_ref), (v_hbm, v_ref)))
    ]
    for copy in copies:
        copy.start()
    for r in range(ROWS):
        all_ref[r, INSIDE:CHANNELS, :] = jnp.ones((CHANNELS - INSIDE, LANES), f32)
    for copy in copies:
        copy.wait()
    for r in range(ROWS):
        all_ref[r, 0:KINDS, :] = y_ref[pl.ds(r, KINDS, stride=ROWS), :]
        all_ref[r, DIFF : DIFF + 1, :] = d_ref[r : r + 1, :]
        all_ref[r, SPEED_C : SPEED_C + 1, :] = v_ref[0, r : r + 1, :]
        all_ref[r, SPEED_R : SPEED_R + 1, :] = v_ref[1, r : r + 1, :]
    odd = lax.axis_index("row") % 2 == 1
    for k in range(STEPS):
        top, bottom = all_ref[k], all_ref[ROWS - STEPS + k]
        near_ref[k] = jnp.where(odd, top, bottom)
        far_ref[k] = jnp.where(odd, bottom, top)


def strip_kernel(all_ref, near_ref, far_ref, done_ref, low_ref, high_ref, left_ref, right_ref):
    odd = lax.axis_index("row") % 2 == 1
    for k in range(STEPS):
        near, far = near_ref[k], far_ref[k]
        low_ref[k] = jnp.where(odd, near, far)
        high_ref[k] = jnp.where(odd, far, near)
    lane = iota((CHANNELS, LANES), 1)
    left = jnp.broadcast_to(done_ref[0:1, :], (CHANNELS, LANES))
    right = jnp.zeros((CHANNELS, LANES), f32)
    for i in range(ROWS + 6):
        plane = low_ref[i] if i < STEPS else all_ref[i - STEPS] if i < STEPS + ROWS else high_ref[i - STEPS - ROWS]
        at = WIDE * i
        left = jnp.where((lane >= at) & (lane < at + WIDE), pltpu.roll(plane, (at + 3) % LANES, 1), left)
        at = (at - 3) % LANES
        hit = (lane - at) % LANES < WIDE
        right = jnp.where(hit, pltpu.roll(plane, (at + 6) % LANES, 1), right)
    left_ref[...] = left
    right_ref[...] = right


def prepare_kernel(
    act_ref, w1_ref, w2_ref, w3_ref, b1_in, b2_in, b3_in, heat_in,
    pick_ref, w1t_ref, w2t_ref, mix_ref, w3t_ref, bias_ref, b1_ref, b2_ref, b3_ref, heat_ref, done_ref,
):
    b1_ref[...] = b1_in[...]
    b2_ref[...] = b2_in[...]
    b3_ref[...] = b3_in[...]
    heat_ref[...] = heat_in[...]
    done_ref[...] = jnp.zeros(done_ref.shape, f32)
    act = act_ref[...].astype(f32)
    before = (iota((LANES, LANES), 0) < iota((LANES, LANES), 1)).astype(f32).astype(bf16)
    inner = jnp.dot(act.astype(bf16), before, preferred_element_type=f32)
    counts = jnp.broadcast_to(jnp.sum(act, axis=1, keepdims=True), (ROWS, LANES))
    row = iota((ROWS, LANES), 0)
    outer = jnp.zeros((ROWS, LANES), f32)
    for k in range(ROWS - 1):
        outer = outer + jnp.where(row > k, jnp.broadcast_to(counts[k : k + 1, :], (ROWS, LANES)), 0.0)
    slot = jnp.where(act > 0.0, inner + outer, -1.0).astype(jnp.int32)
    slots = iota((CAP, LANES), 0)
    for r in range(ROWS):
        hit = slots == jnp.broadcast_to(slot[r : r + 1, :], (CAP, LANES))
        pick_ref[:, r * LANES : (r + 1) * LANES] = jnp.where(hit, 1.0, 0.0).astype(bf16)
    w1t = w1_ref[...].astype(f32)
    w1t_ref[...] = jnp.zeros((2 * CHANNELS, HID), bf16)
    for k in range(2):
        w1t_ref[k * CHANNELS : k * CHANNELS + KINDS + 1, :] = w1t.astype(bf16)
    w2t_ref[...] = w2_ref[...].astype(f32).T.astype(bf16)
    w3t = w3_ref[...].astype(f32).T
    w3t_ref[...] = w3t.astype(bf16)
    part = w1t[0:KINDS, :]
    mix = jnp.dot(w3t.astype(bf16), part.astype(bf16), preferred_element_type=f32)
    mix_ref[...] = (chem_step * mix).astype(bf16)
    shifts = jnp.broadcast_to(b3_in[...], (KINDS, KINDS))
    same = iota((KINDS, KINDS), 0) == iota((KINDS, KINDS), 1)
    shifts = jnp.sum(jnp.where(same, shifts, 0.0), axis=1, keepdims=True)
    bias_ref[...] = chem_step * jnp.sum(part * shifts, axis=0, keepdims=True)


def face(d_low, d_high, u_low, u_high):
    d = 0.5 * (d_low + d_high)
    u = 0.5 * (u_low + u_high)
    return d - jnp.minimum(u, 0.0), d + jnp.maximum(u, 0.0)


def move_kernel(all_ref, low_ref, high_ref, moved_ref, base_ref, coef_ref, one_ref, two_ref):
    ahead, behind = LANES - 1, 1
    for k in range(4):
        base_ref[k, 0:8, :] = jnp.zeros((8, LANES), f32)
        base_ref[k, 22:32, :] = jnp.zeros((10, LANES), f32)
        for i in range(STEPS):
            base_ref[k, 8 + i : 9 + i, :] = low_ref[i, DIFF + k : DIFF + k + 1, :]
            base_ref[k, 19 + i : 20 + i, :] = high_ref[i, DIFF + k : DIFF + k + 1, :]
        for r in range(ROWS):
            base_ref[k, 11 + r : 12 + r, :] = all_ref[r, DIFF + k : DIFF + k + 1, :]
    d, u, v, inside = (base_ref[k, 8:24, :] for k in range(4))
    a_r, b_r = face(d, pltpu.roll(d, ahead, 1), u, pltpu.roll(u, ahead, 1))
    a_l, b_l = pltpu.roll(a_r, behind, 1), pltpu.roll(b_r, behind, 1)
    a_u, b_u = face(d, base_ref[0, 9:25, :], v, base_ref[2, 9:25, :])
    a_d, b_d = face(base_ref[0, 7:23, :], d, base_ref[2, 7:23, :], v)
    for k, c in enumerate((1.0 - b_r - a_l - b_u - a_d, a_r, b_l, a_u, b_d)):
        coef_ref[k] = inside * c

    def load(step, i):
        if step == 0:
            if i < STEPS:
                return low_ref[i, 0:56, :]
            if i < STEPS + ROWS:
                return all_ref[i - STEPS, 0:56, :]
            return high_ref[i - STEPS - ROWS, 0:56, :]
        return (one_ref if step % 2 else two_ref)[i]

    for step in range(STEPS):
        target = two_ref if step % 2 else one_ref
        for i in range(1 + step, 13 - step):
            mine = load(step, i)
            c = [jnp.broadcast_to(coef_ref[k, i : i + 1, :], (56, LANES)) for k in range(5)]
            new = (
                c[0] * mine
                + c[1] * pltpu.roll(mine, ahead, 1)
                + c[2] * pltpu.roll(mine, behind, 1)
                + c[3] * load(step, i + 1)
                + c[4] * load(step, i - 1)
            )
            if step < STEPS - 1:
                target[i] = new
            else:
                moved_ref[i - STEPS] = new


def move_strip(strip):
    ahead, behind = LANES - 1, 1
    d, u, v, inside = (strip[k : k + 1, :] for k in (DIFF, SPEED_C, SPEED_R, INSIDE))
    a_r, b_r = face(d, pltpu.roll(d, ahead, 1), u, pltpu.roll(u, ahead, 1))
    a_l, b_l = pltpu.roll(a_r, behind, 1), pltpu.roll(b_r, behind, 1)
    a_u, b_u = face(d, pltpu.roll(d, LANES - WIDE, 1), v, pltpu.roll(v, LANES - WIDE, 1))
    a_d, b_d = pltpu.roll(a_u, WIDE, 1), pltpu.roll(b_u, WIDE, 1)
    c = [jnp.broadcast_to(inside * x, (56, LANES)) for x in (1.0 - b_r - a_l - b_u - a_d, a_r, b_l, a_u, b_d)]
    strip = strip[0:56, :]
    for _ in range(STEPS):
        strip = (
            c[0] * strip
            + c[1] * pltpu.roll(strip, ahead, 1)
            + c[2] * pltpu.roll(strip, behind, 1)
            + c[3] * pltpu.roll(strip, LANES - WIDE, 1)
            + c[4] * pltpu.roll(strip, WIDE, 1)
        )
    return strip


def main_kernel(
    moved_ref, left_own, right_own, left_ref, right_ref,
    pick_ref, w1t_ref, w2t_ref, mix_ref, w3t_ref, bias_ref, b1_ref, b2_ref, b3_ref, heat_ref,
    out_ref, full_ref, feat_ref, pre_ref, sum_ref,
):
    lane = iota((CHANNELS, LANES), 1)
    left = move_strip(jnp.where(lane % WIDE < 3, left_ref[...], left_own[...]))
    right = move_strip(jnp.where((lane + 3) % LANES % WIDE < 6, right_own[...], right_ref[...]))
    lane = iota((56, LANES), 1)
    place = lane % WIDE
    edges = jnp.where((place >= 3) & (place < 6), left, right)
    outer = (lane < STEPS) | (lane >= LANES - STEPS)
    for r in range(ROWS):
        full_ref[r] = jnp.where(outer, pltpu.roll(edges, (2 * LANES - WIDE * (r + STEPS) - 3) % LANES, 1), moved_ref[r])

    sub = iota((56, LANES), 0)
    for r in range(ROWS):
        block = jnp.where(sub < KINDS, full_ref[r], 0.0)
        block = jnp.where(sub == KINDS, jnp.broadcast_to(heat_ref[r : r + 1, :], (56, LANES)), block)
        block = jnp.concatenate([block, jnp.zeros((8, LANES), f32)], 0)
        coarse = block.astype(bf16)
        fine = jnp.where(iota((CHANNELS, LANES), 0) < KINDS, block - coarse.astype(f32), 0.0).astype(bf16)
        feat_ref[0:CHANNELS, r * LANES : (r + 1) * LANES] = coarse
        feat_ref[CHANNELS:, r * LANES : (r + 1) * LANES] = fine
    slots = lax.dot_general(pick_ref[...], feat_ref[...], (((1,), (1,)), ((), ())), preferred_element_type=f32)
    for k in range(CAP // CHUNK):
        s = slice(k * CHUNK, (k + 1) * CHUNK)
        pre_ref[s, :] = jnp.dot(slots[s, :].astype(bf16), w1t_ref[...], preferred_element_type=f32) + b1_ref[...]
    for index in range(SUBSTEPS):
        for k in range(CAP // CHUNK):
            s = slice(k * CHUNK, (k + 1) * CHUNK)
            first = jnp.tanh(pre_ref[s, :]).astype(bf16)
            second = jnp.dot(first, w2t_ref[...], preferred_element_type=f32) + b2_ref[...]
            second = jnp.tanh(second).astype(bf16)
            wide = second.astype(f32)
            sum_ref[s, :] = wide if index == 0 else sum_ref[s, :] + wide
            if index < SUBSTEPS - 1:
                pre_ref[s, :] += jnp.dot(second, mix_ref[...], preferred_element_type=f32) + bias_ref[...]
    total = sum_ref[...]
    high = total.astype(bf16)
    low = (total - high.astype(f32)).astype(bf16)
    rate = jnp.dot(high, w3t_ref[...], preferred_element_type=f32) + jnp.dot(low, w3t_ref[...], preferred_element_type=f32)
    rate = chem_step * (rate + SUBSTEPS * b3_ref[...])
    rate = jnp.concatenate([rate, jnp.zeros((CAP, LANES - KINDS), f32)], 1).T[0:56, :]
    high = rate.astype(bf16)
    low = (rate - high.astype(f32)).astype(bf16)
    for r in range(ROWS):
        block = pick_ref[:, r * LANES : (r + 1) * LANES]
        gain = jnp.dot(high, block, preferred_element_type=f32) + jnp.dot(low, block, preferred_element_type=f32)
        out_ref[pl.ds(r, KINDS, stride=ROWS), :] = (full_ref[r] + gain)[0:KINDS, :]


def stay(x):
    return pltpu.with_memory_space_constraint(x, pltpu.HBM)


def call(kernel, shapes, operands, name, scratch=(), copies=0, cost=None):
    return pl.pallas_call(
        kernel,
        out_shape=[jax.ShapeDtypeStruct(s, t) for s, t in shapes],
        in_specs=[pl.BlockSpec(memory_space=pltpu.HBM if copies else pltpu.VMEM)] * len(operands),
        out_specs=[pl.BlockSpec(memory_space=pltpu.VMEM)] * len(shapes),
        scratch_shapes=[pltpu.VMEM(s, t) for s, t in scratch] + [pltpu.SemaphoreType.DMA((copies,))] * (copies > 0),
        compiler_params=pltpu.CompilerParams(vmem_limit_bytes=16 << 20),
        cost_estimate=cost and pl.CostEstimate(flops=cost, bytes_accessed=0, transcendentals=0),
        name=name,
    )(*operands)


def shards(y, d, v, heat, active, w1, b1, w2, b2, w3, b3):
    plane = (CHANNELS, LANES)
    edge = ((STEPS,) + plane, f32)
    tile = (ROWS, LANES)
    every, near, far = call(
        planes_kernel, [((ROWS,) + plane, f32), edge, edge], [stay(x) for x in (y.reshape(KINDS * ROWS, LANES), d, v)], "planes",
        scratch=[((KINDS * ROWS, LANES), f32), (tile, f32), ((2,) + tile, f32)], copies=3,
    )
    devices = lax.axis_size("row")
    far = lax.ppermute(far, "row", [(i, i + 1 if i % 2 else i - 1) for i in range(1, devices - 1)])
    near = lax.ppermute(near, "row", [(i, i ^ 1) for i in range(devices)])
    *picks, done = call(
        prepare_kernel,
        [
            ((CAP, ROWS * LANES), bf16), ((2 * CHANNELS, HID), bf16), ((HID, HID), bf16), ((HID, HID), bf16),
            ((HID, KINDS), bf16), ((1, HID), f32), ((1, HID), f32), ((1, HID), f32), ((1, KINDS), f32), (tile, f32),
            (tile, f32),
        ],
        (active, w1.T, w2, w3, b1[None], b2[None], b3[None], heat),
        "prepare",
        cost=COST_PREPARE,
    )
    low, high, left_own, right_own = call(
        strip_kernel, [edge, edge, (plane, f32), (plane, f32)], (every, near, far, done), "strip"
    )
    devices = lax.axis_size("col")
    up = [(i, i + 1) for i in range(devices - 1)]
    left = lax.ppermute(left_own, "col", up)
    right = lax.ppermute(right_own, "col", [(b, a) for a, b in up])
    (moved,) = call(
        move_kernel, [((ROWS, 56, LANES), f32)], (every, low, high), "move",
        scratch=[((4, 32, LANES), f32), ((5, 16, LANES), f32), ((14, 56, LANES), f32), ((14, 56, LANES), f32)],
        cost=COST_MOVE,
    )
    (out,) = call(
        main_kernel,
        [((KINDS * ROWS, LANES), f32)],
        (moved, left_own, right_own, left, right, *picks),
        "main",
        scratch=[
            ((ROWS, 56, LANES), f32), ((2 * CHANNELS, ROWS * LANES), bf16), ((CAP, HID), f32), ((CAP, HID), f32),
        ],
    )
    return out.reshape(KINDS, ROWS, LANES)


def solution(mesh):
    tile, rest = P("row", "col"), P()
    stack = P(None, "row", "col")
    in_specs = (stack, tile, stack, tile, tile, rest, rest, rest, rest, rest, rest)
    return jax.shard_map(shards, mesh=mesh, in_specs=in_specs, out_specs=stack, check_vma=False)
```

```python
import jax
import jax.numpy as jnp
from jax import lax
from jax.experimental import pallas as pl
from jax.experimental.pallas import tpu as pltpu
from jax.sharding import PartitionSpec as P


SUBSTEPS = 8
STEPS = 3
KINDS = 54
HID = 256
ROWS = 8
LANES = 128
CAP = 384
CHUNK = 128
CHANNELS = 64
DIFF, SPEED_C, SPEED_R, INSIDE = 54, 55, 56, 57
WIDE = 9
COST_PREPARE = 20_000_000
COST_MOVE = 20_000_000
chem_step = 0.0625
f32 = jnp.float32
bf16 = jnp.bfloat16


def iota(shape, axis):
    return lax.broadcasted_iota(jnp.int32, shape, axis)


def planes_kernel(y_hbm, d_hbm, v_hbm, all_ref, near_ref, far_ref, y_ref, d_ref, v_ref, sems):
    copies = [
        pltpu.make_async_copy(source, target, sems.at[k])
        for k, (source, target) in enumerate(((y_hbm, y_ref), (d_hbm, d_ref), (v_hbm, v_ref)))
    ]
    for copy in copies:
        copy.start()
    for r in range(ROWS):
        all_ref[r, INSIDE:CHANNELS, :] = jnp.ones((CHANNELS - INSIDE, LANES), f32)
    for copy in copies:
        copy.wait()
    for r in range(ROWS):
        all_ref[r, 0:KINDS, :] = y_ref[pl.ds(r, KINDS, stride=ROWS), :]
        all_ref[r, DIFF : DIFF + 1, :] = d_ref[r : r + 1, :]
        all_ref[r, SPEED_C : SPEED_C + 1, :] = v_ref[0, r : r + 1, :]
        all_ref[r, SPEED_R : SPEED_R + 1, :] = v_ref[1, r : r + 1, :]
    odd = lax.axis_index("row") % 2 == 1
    for k in range(STEPS):
        top, bottom = all_ref[k], all_ref[ROWS - STEPS + k]
        near_ref[k] = jnp.where(odd, top, bottom)
        far_ref[k] = jnp.where(odd, bottom, top)


def strip_kernel(all_ref, near_ref, far_ref, done_ref, low_ref, high_ref, left_ref, right_ref):
    odd = lax.axis_index("row") % 2 == 1
    for k in range(STEPS):
        near, far = near_ref[k], far_ref[k]
        low_ref[k] = jnp.where(odd, near, far)
        high_ref[k] = jnp.where(odd, far, near)
    lane = iota((CHANNELS, LANES), 1)
    left = jnp.broadcast_to(done_ref[0:1, :], (CHANNELS, LANES))
    right = jnp.zeros((CHANNELS, LANES), f32)
    for i in range(ROWS + 6):
        plane = low_ref[i] if i < STEPS else all_ref[i - STEPS] if i < STEPS + ROWS else high_ref[i - STEPS - ROWS]
        at = WIDE * i
        left = jnp.where((lane >= at) & (lane < at + WIDE), pltpu.roll(plane, (at + 3) % LANES, 1), left)
        at = (at - 3) % LANES
        hit = (lane - at) % LANES < WIDE
        right = jnp.where(hit, pltpu.roll(plane, (at + 6) % LANES, 1), right)
    left_ref[...] = left
    right_ref[...] = right


def prepare_kernel(
    act_ref, w1_ref, w2_ref, w3_ref, b1_in, b2_in, b3_in, heat_in,
    pick_ref, w1t_ref, w2t_ref, mix_ref, w3t_ref, bias_ref, b1_ref, b2_ref, b3_ref, heat_ref, done_ref,
):
    b1_ref[...] = b1_in[...]
    b2_ref[...] = b2_in[...]
    b3_ref[...] = b3_in[...]
    heat_ref[...] = heat_in[...]
    done_ref[...] = jnp.zeros(done_ref.shape, f32)
    act = act_ref[...].astype(f32)
    before = (iota((LANES, LANES), 0) < iota((LANES, LANES), 1)).astype(f32).astype(bf16)
    inner = jnp.dot(act.astype(bf16), before, preferred_element_type=f32)
    counts = jnp.broadcast_to(jnp.sum(act, axis=1, keepdims=True), (ROWS, LANES))
    row = iota((ROWS, LANES), 0)
    outer = jnp.zeros((ROWS, LANES), f32)
    for k in range(ROWS - 1):
        outer = outer + jnp.where(row > k, jnp.broadcast_to(counts[k : k + 1, :], (ROWS, LANES)), 0.0)
    slot = jnp.where(act > 0.0, inner + outer, -1.0).astype(jnp.int32)
    slots = iota((CAP, LANES), 0)
    for r in range(ROWS):
        hit = slots == jnp.broadcast_to(slot[r : r + 1, :], (CAP, LANES))
        pick_ref[:, r * LANES : (r + 1) * LANES] = jnp.where(hit, 1.0, 0.0).astype(bf16)
    w1t = w1_ref[...].astype(f32)
    w1t_ref[...] = jnp.zeros((2 * CHANNELS, HID), bf16)
    for k in range(2):
        w1t_ref[k * CHANNELS : k * CHANNELS + KINDS + 1, :] = w1t.astype(bf16)
    w2t_ref[...] = w2_ref[...].astype(f32).T.astype(bf16)
    w3t = w3_ref[...].astype(f32).T
    w3t_ref[...] = w3t.astype(bf16)
    part = w1t[0:KINDS, :]
    mix = jnp.dot(w3t.astype(bf16), part.astype(bf16), preferred_element_type=f32)
    mix_ref[...] = (chem_step * mix).astype(bf16)
    shifts = jnp.broadcast_to(b3_in[...], (KINDS, KINDS))
    same = iota((KINDS, KINDS), 0) == iota((KINDS, KINDS), 1)
    shifts = jnp.sum(jnp.where(same, shifts, 0.0), axis=1, keepdims=True)
    bias_ref[...] = chem_step * jnp.sum(part * shifts, axis=0, keepdims=True)


def face(d_low, d_high, u_low, u_high):
    d = 0.5 * (d_low + d_high)
    u = 0.5 * (u_low + u_high)
    return d - jnp.minimum(u, 0.0), d + jnp.maximum(u, 0.0)


def move_kernel(all_ref, low_ref, high_ref, moved_ref, base_ref, coef_ref, one_ref, two_ref):
    ahead, behind = LANES - 1, 1
    for k in range(4):
        base_ref[k, 0:8, :] = jnp.zeros((8, LANES), f32)
        base_ref[k, 22:32, :] = jnp.zeros((10, LANES), f32)
        for i in range(STEPS):
            base_ref[k, 8 + i : 9 + i, :] = low_ref[i, DIFF + k : DIFF + k + 1, :]
            base_ref[k, 19 + i : 20 + i, :] = high_ref[i, DIFF + k : DIFF + k + 1, :]
        for r in range(ROWS):
            base_ref[k, 11 + r : 12 + r, :] = all_ref[r, DIFF + k : DIFF + k + 1, :]
    d, u, v, inside = (base_ref[k, 8:24, :] for k in range(4))
    a_r, b_r = face(d, pltpu.roll(d, ahead, 1), u, pltpu.roll(u, ahead, 1))
    a_l, b_l = pltpu.roll(a_r, behind, 1), pltpu.roll(b_r, behind, 1)
    a_u, b_u = face(d, base_ref[0, 9:25, :], v, base_ref[2, 9:25, :])
    a_d, b_d = face(base_ref[0, 7:23, :], d, base_ref[2, 7:23, :], v)
    for k, c in enumerate((1.0 - b_r - a_l - b_u - a_d, a_r, b_l, a_u, b_d)):
        coef_ref[k] = inside * c

    def load(step, i):
        if step == 0:
            if i < STEPS:
                return low_ref[i, 0:56, :]
            if i < STEPS + ROWS:
                return all_ref[i - STEPS, 0:56, :]
            return high_ref[i - STEPS - ROWS, 0:56, :]
        return (one_ref if step % 2 else two_ref)[i]

    for step in range(STEPS):
        target = two_ref if step % 2 else one_ref
        for i in range(1 + step, 13 - step):
            mine = load(step, i)
            c = [jnp.broadcast_to(coef_ref[k, i : i + 1, :], (56, LANES)) for k in range(5)]
            new = (
                c[0] * mine
                + c[1] * pltpu.roll(mine, ahead, 1)
                + c[2] * pltpu.roll(mine, behind, 1)
                + c[3] * load(step, i + 1)
                + c[4] * load(step, i - 1)
            )
            if step < STEPS - 1:
                target[i] = new
            else:
                moved_ref[i - STEPS] = new


def move_strip(strip):
    ahead, behind = LANES - 1, 1
    d, u, v, inside = (strip[k : k + 1, :] for k in (DIFF, SPEED_C, SPEED_R, INSIDE))
    a_r, b_r = face(d, pltpu.roll(d, ahead, 1), u, pltpu.roll(u, ahead, 1))
    a_l, b_l = pltpu.roll(a_r, behind, 1), pltpu.roll(b_r, behind, 1)
    a_u, b_u = face(d, pltpu.roll(d, LANES - WIDE, 1), v, pltpu.roll(v, LANES - WIDE, 1))
    a_d, b_d = pltpu.roll(a_u, WIDE, 1), pltpu.roll(b_u, WIDE, 1)
    c = [jnp.broadcast_to(inside * x, (56, LANES)) for x in (1.0 - b_r - a_l - b_u - a_d, a_r, b_l, a_u, b_d)]
    strip = strip[0:56, :]
    for _ in range(STEPS):
        strip = (
            c[0] * strip
            + c[1] * pltpu.roll(strip, ahead, 1)
            + c[2] * pltpu.roll(strip, behind, 1)
            + c[3] * pltpu.roll(strip, LANES - WIDE, 1)
            + c[4] * pltpu.roll(strip, WIDE, 1)
        )
    return strip


def main_kernel(
    moved_ref, left_own, right_own, left_ref, right_ref,
    pick_ref, w1t_ref, w2t_ref, mix_ref, w3t_ref, bias_ref, b1_ref, b2_ref, b3_ref, heat_ref,
    out_ref, full_ref, feat_ref, pre_ref, sum_ref,
):
    lane = iota((CHANNELS, LANES), 1)
    left = move_strip(jnp.where(lane % WIDE < 3, left_ref[...], left_own[...]))
    right = move_strip(jnp.where((lane + 3) % LANES % WIDE < 6, right_own[...], right_ref[...]))
    lane = iota((56, LANES), 1)
    place = lane % WIDE
    edges = jnp.where((place >= 3) & (place < 6), left, right)
    outer = (lane < STEPS) | (lane >= LANES - STEPS)
    for r in range(ROWS):
        full_ref[r] = jnp.where(outer, pltpu.roll(edges, (2 * LANES - WIDE * (r + STEPS) - 3) % LANES, 1), moved_ref[r])

    sub = iota((56, LANES), 0)
    for r in range(ROWS):
        block = jnp.where(sub < KINDS, full_ref[r], 0.0)
        block = jnp.where(sub == KINDS, jnp.broadcast_to(heat_ref[r : r + 1, :], (56, LANES)), block)
        block = jnp.concatenate([block, jnp.zeros((8, LANES), f32)], 0)
        coarse = block.astype(bf16)
        fine = jnp.where(iota((CHANNELS, LANES), 0) < KINDS, block - coarse.astype(f32), 0.0).astype(bf16)
        feat_ref[0:CHANNELS, r * LANES : (r + 1) * LANES] = coarse
        feat_ref[CHANNELS:, r * LANES : (r + 1) * LANES] = fine
    slots = lax.dot_general(pick_ref[...], feat_ref[...], (((1,), (1,)), ((), ())), preferred_element_type=f32)
    for k in range(CAP // CHUNK):
        s = slice(k * CHUNK, (k + 1) * CHUNK)
        pre_ref[s, :] = jnp.dot(slots[s, :].astype(bf16), w1t_ref[...], preferred_element_type=f32) + b1_ref[...]
    for index in range(SUBSTEPS):
        for k in range(CAP // CHUNK):
            s = slice(k * CHUNK, (k + 1) * CHUNK)
            first = jnp.tanh(pre_ref[s, :]).astype(bf16)
            second = jnp.dot(first, w2t_ref[...], preferred_element_type=f32) + b2_ref[...]
            second = jnp.tanh(second).astype(bf16)
            wide = second.astype(f32)
            sum_ref[s, :] = wide if index == 0 else sum_ref[s, :] + wide
            if index < SUBSTEPS - 1:
                pre_ref[s, :] += jnp.dot(second, mix_ref[...], preferred_element_type=f32) + bias_ref[...]
    total = sum_ref[...]
    high = total.astype(bf16)
    low = (total - high.astype(f32)).astype(bf16)
    rate = jnp.dot(high, w3t_ref[...], preferred_element_type=f32) + jnp.dot(low, w3t_ref[...], preferred_element_type=f32)
    rate = chem_step * (rate + SUBSTEPS * b3_ref[...])
    rate = jnp.concatenate([rate, jnp.zeros((CAP, LANES - KINDS), f32)], 1).T[0:56, :]
    high = rate.astype(bf16)
    low = (rate - high.astype(f32)).astype(bf16)
    for r in range(ROWS):
        block = pick_ref[:, r * LANES : (r + 1) * LANES]
        gain = jnp.dot(high, block, preferred_element_type=f32) + jnp.dot(low, block, preferred_element_type=f32)
        out_ref[pl.ds(r, KINDS, stride=ROWS), :] = (full_ref[r] + gain)[0:KINDS, :]


def stay(x):
    return pltpu.with_memory_space_constraint(x, pltpu.HBM)


def call(kernel, shapes, operands, scratch=(), copies=0, cost=None):
    return pl.pallas_call(
        kernel,
        out_shape=[jax.ShapeDtypeStruct(s, t) for s, t in shapes],
        in_specs=[pl.BlockSpec(memory_space=pltpu.HBM if copies else pltpu.VMEM)] * len(operands),
        out_specs=[pl.BlockSpec(memory_space=pltpu.VMEM)] * len(shapes),
        scratch_shapes=[pltpu.VMEM(s, t) for s, t in scratch] + [pltpu.SemaphoreType.DMA((copies,))] * (copies > 0),
        compiler_params=pltpu.CompilerParams(vmem_limit_bytes=16 << 20),
        cost_estimate=cost and pl.CostEstimate(flops=cost, bytes_accessed=0, transcendentals=0),
    )(*operands)


def shards(y, d, v, heat, active, w1, b1, w2, b2, w3, b3):
    plane = (CHANNELS, LANES)
    edge = ((STEPS,) + plane, f32)
    tile = (ROWS, LANES)
    every, near, far = call(
        planes_kernel, [((ROWS,) + plane, f32), edge, edge], [stay(x) for x in (y.reshape(KINDS * ROWS, LANES), d, v)],
        scratch=[((KINDS * ROWS, LANES), f32), (tile, f32), ((2,) + tile, f32)], copies=3,
    )
    devices = lax.axis_size("row")
    far = lax.ppermute(far, "row", [(i, i + 1 if i % 2 else i - 1) for i in range(1, devices - 1)])
    near = lax.ppermute(near, "row", [(i, i ^ 1) for i in range(devices)])
    *picks, done = call(
        prepare_kernel,
        [
            ((CAP, ROWS * LANES), bf16), ((2 * CHANNELS, HID), bf16), ((HID, HID), bf16), ((HID, HID), bf16),
            ((HID, KINDS), bf16), ((1, HID), f32), ((1, HID), f32), ((1, HID), f32), ((1, KINDS), f32), (tile, f32),
            (tile, f32),
        ],
        (active, w1.T, w2, w3, b1[None], b2[None], b3[None], heat),
        cost=COST_PREPARE,
    )
    low, high, left_own, right_own = call(
        strip_kernel, [edge, edge, (plane, f32), (plane, f32)], (every, near, far, done)
    )
    devices = lax.axis_size("col")
    up = [(i, i + 1) for i in range(devices - 1)]
    right = lax.ppermute(right_own, "col", [(b, a) for a, b in up])
    left = lax.ppermute(left_own, "col", up)
    (moved,) = call(
        move_kernel, [((ROWS, 56, LANES), f32)], (every, low, high),
        scratch=[((4, 32, LANES), f32), ((5, 16, LANES), f32), ((14, 56, LANES), f32), ((14, 56, LANES), f32)],
        cost=COST_MOVE,
    )
    (out,) = call(
        main_kernel,
        [((KINDS * ROWS, LANES), f32)],
        (moved, left_own, right_own, left, right, *picks),
        scratch=[
            ((ROWS, 56, LANES), f32), ((2 * CHANNELS, ROWS * LANES), bf16), ((CAP, HID), f32), ((CAP, HID), f32),
        ],
    )
    return out.reshape(KINDS, ROWS, LANES)


def solution(mesh):
    tile, rest = P("row", "col"), P()
    stack = P(None, "row", "col")
    in_specs = (stack, tile, stack, tile, tile, rest, rest, rest, rest, rest, rest)
    return jax.shard_map(shards, mesh=mesh, in_specs=in_specs, out_specs=stack, check_vma=False)
```

```python
import jax
import jax.numpy as jnp
from jax import lax
from jax.experimental import pallas as pl
from jax.experimental.pallas import tpu as pltpu
from jax.sharding import PartitionSpec as P


SUBSTEPS = 8
STEPS = 3
KINDS = 54
HID = 256
ROWS = 8
LANES = 128
CAP = 384
CHUNK = 192
CHANNELS = 64
DIFF, SPEED_C, SPEED_R, INSIDE = 54, 55, 56, 57
WIDE = 9
COST_PREPARE = 20_000_000
COST_MOVE = 20_000_000
chem_step = 0.0625
f32 = jnp.float32
bf16 = jnp.bfloat16


def iota(shape, axis):
    return lax.broadcasted_iota(jnp.int32, shape, axis)


def planes_kernel(
    y_hbm, d_hbm, v_hbm, act_hbm, heat_hbm, b1_hbm, b2_hbm, b3_hbm,
    all_ref, near_ref, far_ref, act_ref, heat_ref, b1_ref, b2_ref, b3_ref, y_ref, d_ref, v_ref, sems,
):
    pairs = (
        (y_hbm, y_ref), (d_hbm, d_ref), (v_hbm, v_ref), (act_hbm, act_ref), (heat_hbm, heat_ref),
        (b1_hbm, b1_ref), (b2_hbm, b2_ref), (b3_hbm, b3_ref),
    )
    copies = [pltpu.make_async_copy(source, target, sems.at[k]) for k, (source, target) in enumerate(pairs)]
    for copy in copies:
        copy.start()
    for r in range(ROWS):
        all_ref[r, INSIDE:CHANNELS, :] = jnp.ones((CHANNELS - INSIDE, LANES), f32)
    for copy in copies:
        copy.wait()
    for r in range(ROWS):
        all_ref[r, 0:KINDS, :] = y_ref[pl.ds(r, KINDS, stride=ROWS), :]
        all_ref[r, DIFF : DIFF + 1, :] = d_ref[r : r + 1, :]
        all_ref[r, SPEED_C : SPEED_C + 1, :] = v_ref[0, r : r + 1, :]
        all_ref[r, SPEED_R : SPEED_R + 1, :] = v_ref[1, r : r + 1, :]
    odd = lax.axis_index("row") % 2 == 1
    for k in range(STEPS):
        top, bottom = all_ref[k], all_ref[ROWS - STEPS + k]
        near_ref[k] = jnp.where(odd, top, bottom)
        far_ref[k] = jnp.where(odd, bottom, top)


def strip_kernel(all_ref, near_ref, far_ref, token_ref, low_ref, high_ref, first_ref, second_ref):
    odd = lax.axis_index("row") % 2 == 1
    for k in range(STEPS):
        near, far = near_ref[k], far_ref[k]
        low_ref[k] = jnp.where(odd, near, far)
        high_ref[k] = jnp.where(odd, far, near)
    lane = iota((CHANNELS, LANES), 1)
    left = jnp.broadcast_to(token_ref[0:1, :], (CHANNELS, LANES))
    right = jnp.zeros((CHANNELS, LANES), f32)
    for i in range(ROWS + 6):
        plane = low_ref[i] if i < STEPS else all_ref[i - STEPS] if i < STEPS + ROWS else high_ref[i - STEPS - ROWS]
        at = WIDE * i
        left = jnp.where((lane >= at) & (lane < at + WIDE), pltpu.roll(plane, (at + 3) % LANES, 1), left)
        at = (at - 3) % LANES
        hit = (lane - at) % LANES < WIDE
        right = jnp.where(hit, pltpu.roll(plane, (at + 6) % LANES, 1), right)
    odd = lax.axis_index("col") % 2 == 1
    first_ref[...] = jnp.where(odd, right, left)
    second_ref[...] = jnp.where(odd, left, right)


def prepare_kernel(
    act_ref, w1_ref, w2_ref, w3_ref, b3_ref, pick_ref, w1t_ref, w2t_ref, mix_ref, w3t_ref, bias_ref, token_ref
):
    token_ref[...] = jnp.zeros(token_ref.shape, f32)
    act = act_ref[...].astype(f32)
    before = (iota((LANES, LANES), 0) < iota((LANES, LANES), 1)).astype(f32).astype(bf16)
    inner = jnp.dot(act.astype(bf16), before, preferred_element_type=f32)
    counts = jnp.broadcast_to(jnp.sum(act, axis=1, keepdims=True), (ROWS, LANES))
    row = iota((ROWS, LANES), 0)
    outer = jnp.zeros((ROWS, LANES), f32)
    for k in range(ROWS - 1):
        outer = outer + jnp.where(row > k, jnp.broadcast_to(counts[k : k + 1, :], (ROWS, LANES)), 0.0)
    slot = jnp.where(act > 0.0, inner + outer, -1.0).astype(jnp.int32)
    slots = iota((CAP, LANES), 0)
    for r in range(ROWS):
        hit = slots == jnp.broadcast_to(slot[r : r + 1, :], (CAP, LANES))
        pick_ref[:, r * LANES : (r + 1) * LANES] = jnp.where(hit, 1.0, 0.0).astype(bf16)
    w1t = w1_ref[...].astype(f32)
    w1t_ref[...] = jnp.zeros((2 * CHANNELS, HID), bf16)
    for k in range(2):
        w1t_ref[k * CHANNELS : k * CHANNELS + KINDS + 1, :] = w1t.astype(bf16)
    w2t_ref[...] = w2_ref[...].astype(f32).T.astype(bf16)
    w3t = w3_ref[...].astype(f32).T
    w3t_ref[...] = w3t.astype(bf16)
    part = w1t[0:KINDS, :]
    mix = jnp.dot(w3t.astype(bf16), part.astype(bf16), preferred_element_type=f32)
    mix_ref[...] = (chem_step * mix).astype(bf16)
    shifts = jnp.broadcast_to(b3_ref[...], (KINDS, KINDS))
    same = iota((KINDS, KINDS), 0) == iota((KINDS, KINDS), 1)
    shifts = jnp.sum(jnp.where(same, shifts, 0.0), axis=1, keepdims=True)
    bias_ref[...] = chem_step * jnp.sum(part * shifts, axis=0, keepdims=True)


def face(d_low, d_high, u_low, u_high):
    d = 0.5 * (d_low + d_high)
    u = 0.5 * (u_low + u_high)
    return d - jnp.minimum(u, 0.0), d + jnp.maximum(u, 0.0)


def move_kernel(all_ref, low_ref, high_ref, moved_ref, base_ref, coef_ref, one_ref, two_ref):
    ahead, behind = LANES - 1, 1
    for k in range(4):
        base_ref[k, 0:8, :] = jnp.zeros((8, LANES), f32)
        base_ref[k, 22:32, :] = jnp.zeros((10, LANES), f32)
        for i in range(STEPS):
            base_ref[k, 8 + i : 9 + i, :] = low_ref[i, DIFF + k : DIFF + k + 1, :]
            base_ref[k, 19 + i : 20 + i, :] = high_ref[i, DIFF + k : DIFF + k + 1, :]
        for r in range(ROWS):
            base_ref[k, 11 + r : 12 + r, :] = all_ref[r, DIFF + k : DIFF + k + 1, :]
    d, u, v, inside = (base_ref[k, 8:24, :] for k in range(4))
    a_r, b_r = face(d, pltpu.roll(d, ahead, 1), u, pltpu.roll(u, ahead, 1))
    a_l, b_l = pltpu.roll(a_r, behind, 1), pltpu.roll(b_r, behind, 1)
    a_u, b_u = face(d, base_ref[0, 9:25, :], v, base_ref[2, 9:25, :])
    a_d, b_d = face(base_ref[0, 7:23, :], d, base_ref[2, 7:23, :], v)
    for k, c in enumerate((1.0 - b_r - a_l - b_u - a_d, a_r, b_l, a_u, b_d)):
        coef_ref[k] = inside * c

    def load(step, i):
        if step == 0:
            if i < STEPS:
                return low_ref[i, 0:56, :]
            if i < STEPS + ROWS:
                return all_ref[i - STEPS, 0:56, :]
            return high_ref[i - STEPS - ROWS, 0:56, :]
        return (one_ref if step % 2 else two_ref)[i]

    for step in range(STEPS):
        target = two_ref if step % 2 else one_ref
        for i in range(1 + step, 13 - step):
            mine = load(step, i)
            c = [jnp.broadcast_to(coef_ref[k, i : i + 1, :], (56, LANES)) for k in range(5)]
            new = (
                c[0] * mine
                + c[1] * pltpu.roll(mine, ahead, 1)
                + c[2] * pltpu.roll(mine, behind, 1)
                + c[3] * load(step, i + 1)
                + c[4] * load(step, i - 1)
            )
            if step < STEPS - 1:
                target[i] = new
            else:
                moved_ref[i - STEPS] = new


def move_strip(strip):
    ahead, behind = LANES - 1, 1
    d, u, v, inside = (strip[k : k + 1, :] for k in (DIFF, SPEED_C, SPEED_R, INSIDE))
    a_r, b_r = face(d, pltpu.roll(d, ahead, 1), u, pltpu.roll(u, ahead, 1))
    a_l, b_l = pltpu.roll(a_r, behind, 1), pltpu.roll(b_r, behind, 1)
    a_u, b_u = face(d, pltpu.roll(d, LANES - WIDE, 1), v, pltpu.roll(v, LANES - WIDE, 1))
    a_d, b_d = pltpu.roll(a_u, WIDE, 1), pltpu.roll(b_u, WIDE, 1)
    c = [jnp.broadcast_to(inside * x, (56, LANES)) for x in (1.0 - b_r - a_l - b_u - a_d, a_r, b_l, a_u, b_d)]
    strip = strip[0:56, :]
    for _ in range(STEPS):
        strip = (
            c[0] * strip
            + c[1] * pltpu.roll(strip, ahead, 1)
            + c[2] * pltpu.roll(strip, behind, 1)
            + c[3] * pltpu.roll(strip, LANES - WIDE, 1)
            + c[4] * pltpu.roll(strip, WIDE, 1)
        )
    return strip


def main_kernel(
    moved_ref, first_ref, second_ref, early_ref, late_ref,
    pick_ref, w1t_ref, w2t_ref, mix_ref, w3t_ref, bias_ref, b1_ref, b2_ref, b3_ref, heat_ref,
    out_ref, full_ref, feat_ref, pre_ref, sum_ref,
):
    lane = iota((CHANNELS, LANES), 1)
    odd = lax.axis_index("col") % 2 == 1
    first, second, early, late = first_ref[...], second_ref[...], early_ref[...], late_ref[...]
    left = jnp.where(lane % WIDE < 3, jnp.where(odd, early, late), jnp.where(odd, second, first))
    inner = (lane + 3) % LANES % WIDE < 6
    right = jnp.where(inner, jnp.where(odd, first, second), jnp.where(odd, late, early))
    left, right = move_strip(left), move_strip(right)
    lane = iota((56, LANES), 1)
    place = lane % WIDE
    edges = jnp.where((place >= 3) & (place < 6), left, right)
    outer = (lane < STEPS) | (lane >= LANES - STEPS)
    for r in range(ROWS):
        full_ref[r] = jnp.where(outer, pltpu.roll(edges, (2 * LANES - WIDE * (r + STEPS) - 3) % LANES, 1), moved_ref[r])

    sub = iota((56, LANES), 0)
    for r in range(ROWS):
        block = jnp.where(sub < KINDS, full_ref[r], 0.0)
        block = jnp.where(sub == KINDS, jnp.broadcast_to(heat_ref[r : r + 1, :], (56, LANES)), block)
        block = jnp.concatenate([block, jnp.zeros((8, LANES), f32)], 0)
        coarse = block.astype(bf16)
        fine = jnp.where(iota((CHANNELS, LANES), 0) < KINDS, block - coarse.astype(f32), 0.0).astype(bf16)
        feat_ref[0:CHANNELS, r * LANES : (r + 1) * LANES] = coarse
        feat_ref[CHANNELS:, r * LANES : (r + 1) * LANES] = fine
    slots = lax.dot_general(pick_ref[...], feat_ref[...], (((1,), (1,)), ((), ())), preferred_element_type=f32)
    for k in range(CAP // CHUNK):
        s = slice(k * CHUNK, (k + 1) * CHUNK)
        pre_ref[s, :] = jnp.dot(slots[s, :].astype(bf16), w1t_ref[...], preferred_element_type=f32) + b1_ref[...]
    parts = [slice(k * CHUNK, (k + 1) * CHUNK) for k in range(CAP // CHUNK)]
    for index in range(SUBSTEPS):
        first = [jnp.tanh(pre_ref[s, :]).astype(bf16) for s in parts]
        second = [jnp.dot(h, w2t_ref[...], preferred_element_type=f32) + b2_ref[...] for h in first]
        second = [jnp.tanh(h).astype(bf16) for h in second]
        for s, h in zip(parts, second):
            wide = h.astype(f32)
            sum_ref[s, :] = wide if index == 0 else sum_ref[s, :] + wide
            if index < SUBSTEPS - 1:
                pre_ref[s, :] += jnp.dot(h, mix_ref[...], preferred_element_type=f32) + bias_ref[...]
    total = sum_ref[...]
    high = total.astype(bf16)
    low = (total - high.astype(f32)).astype(bf16)
    rate = jnp.dot(high, w3t_ref[...], preferred_element_type=f32) + jnp.dot(low, w3t_ref[...], preferred_element_type=f32)
    rate = chem_step * (rate + SUBSTEPS * b3_ref[...])
    rate = jnp.concatenate([rate, jnp.zeros((CAP, LANES - KINDS), f32)], 1).T[0:CHANNELS, :]
    high = rate.astype(bf16)
    low = (rate - high.astype(f32)).astype(bf16)
    both = jnp.concatenate([high, low], 0)
    for r in range(0, ROWS, 2):
        gain = jnp.dot(both, pick_ref[:, r * LANES : (r + 2) * LANES], preferred_element_type=f32)
        gain = gain[0:CHANNELS] + gain[CHANNELS:]
        for k in range(2):
            block = full_ref[r + k] + gain[0:56, k * LANES : (k + 1) * LANES]
            out_ref[pl.ds(r + k, KINDS, stride=ROWS), :] = block[0:KINDS]


def stay(x):
    return pltpu.with_memory_space_constraint(x, pltpu.HBM)


def call(kernel, shapes, operands, scratch=(), copies=0, cost=None):
    return pl.pallas_call(
        kernel,
        out_shape=[jax.ShapeDtypeStruct(s, t) for s, t in shapes],
        in_specs=[pl.BlockSpec(memory_space=pltpu.HBM if copies else pltpu.VMEM)] * len(operands),
        out_specs=[pl.BlockSpec(memory_space=pltpu.VMEM)] * len(shapes),
        scratch_shapes=[pltpu.VMEM(s, t) for s, t in scratch] + [pltpu.SemaphoreType.DMA((copies,))] * (copies > 0),
        compiler_params=pltpu.CompilerParams(vmem_limit_bytes=16 << 20),
        cost_estimate=cost and pl.CostEstimate(flops=cost, bytes_accessed=0, transcendentals=0),
    )(*operands)


def swaps(devices, first):
    low = range(first, devices - 1, 2)
    return [(i, i + 1) for i in low] + [(i + 1, i) for i in low]


def shards(y, d, v, heat, active, w1, b1, w2, b2, w3, b3):
    plane = (CHANNELS, LANES)
    edge = ((STEPS,) + plane, f32)
    tile = (ROWS, LANES)
    every, near, far, active, heat, b1, b2, b3 = call(
        planes_kernel,
        [
            ((ROWS,) + plane, f32), edge, edge, (tile, jnp.int32), (tile, f32),
            ((1, HID), f32), ((1, HID), f32), ((1, KINDS), f32),
        ],
        [stay(x) for x in (y.reshape(KINDS * ROWS, LANES), d, v, active, heat, b1[None], b2[None], b3[None])],
        scratch=[((KINDS * ROWS, LANES), f32), (tile, f32), ((2,) + tile, f32)], copies=8,
    )
    devices = lax.axis_size("row")
    far = lax.ppermute(far, "row", swaps(devices, 1))
    near = lax.ppermute(near, "row", swaps(devices, 0))
    *picks, token = call(
        prepare_kernel,
        [
            ((CAP, ROWS * LANES), bf16), ((2 * CHANNELS, HID), bf16), ((HID, HID), bf16), ((HID, HID), bf16),
            ((HID, KINDS), bf16), ((1, HID), f32), (tile, f32),
        ],
        (active, w1.T, w2, w3, b3),
        cost=COST_PREPARE,
    )
    low, high, first, second = call(strip_kernel, [edge, edge, (plane, f32), (plane, f32)], (every, near, far, token))
    devices = lax.axis_size("col")
    early = lax.ppermute(first, "col", swaps(devices, 0))
    late = lax.ppermute(second, "col", swaps(devices, 1))
    (moved,) = call(
        move_kernel, [((ROWS, 56, LANES), f32)], (every, low, high),
        scratch=[((4, 32, LANES), f32), ((5, 16, LANES), f32), ((14, 56, LANES), f32), ((14, 56, LANES), f32)],
        cost=COST_MOVE,
    )
    (out,) = call(
        main_kernel,
        [((KINDS * ROWS, LANES), f32)],
        (moved, first, second, early, late, *picks, b1, b2, b3, heat),
        scratch=[
            ((ROWS, 56, LANES), f32), ((2 * CHANNELS, ROWS * LANES), bf16), ((CAP, HID), f32), ((CAP, HID), f32),
        ],
    )
    return out.reshape(KINDS, ROWS, LANES)


def solution(mesh):
    tile, rest = P("row", "col"), P()
    stack = P(None, "row", "col")
    in_specs = (stack, tile, stack, tile, tile, rest, rest, rest, rest, rest, rest)
    return jax.shard_map(shards, mesh=mesh, in_specs=in_specs, out_specs=stack, check_vma=False)
```

```python
import jax
import jax.numpy as jnp
from jax import lax
from jax.experimental import pallas as pl
from jax.experimental.pallas import tpu as pltpu
from jax.sharding import PartitionSpec as P


SUBSTEPS = 8
STEPS = 3
KINDS = 54
HID = 256
ROWS = 8
LANES = 128
CAP = 384
CHUNK = 192
CHANNELS = 64
DIFF, SPEED_C, SPEED_R, INSIDE = 54, 55, 56, 57
WIDE = 9
PACK = 24
COST_PREPARE = 20_000_000
COST_MOVE = 20_000_000
chem_step = 0.0625
f32 = jnp.float32
bf16 = jnp.bfloat16


def iota(shape, axis):
    return lax.broadcasted_iota(jnp.int32, shape, axis)


def planes_kernel(
    y_hbm, d_hbm, v_hbm, act_hbm, heat_hbm, b1_hbm, b2_hbm, b3_hbm,
    all_ref, near_ref, far_ref, act_ref, heat_ref, b1_ref, b2_ref, b3_ref, y_ref, d_ref, v_ref, sems,
):
    pairs = (
        (y_hbm, y_ref), (d_hbm, d_ref), (v_hbm, v_ref), (act_hbm, act_ref), (heat_hbm, heat_ref),
        (b1_hbm, b1_ref), (b2_hbm, b2_ref), (b3_hbm, b3_ref),
    )
    copies = [pltpu.make_async_copy(source, target, sems.at[k]) for k, (source, target) in enumerate(pairs)]
    for copy in copies:
        copy.start()
    for r in range(ROWS):
        all_ref[r, INSIDE:CHANNELS, :] = jnp.ones((CHANNELS - INSIDE, LANES), f32)
    for copy in copies:
        copy.wait()
    for r in range(ROWS):
        all_ref[r, 0:KINDS, :] = y_ref[pl.ds(r, KINDS, stride=ROWS), :]
        all_ref[r, DIFF : DIFF + 1, :] = d_ref[r : r + 1, :]
        all_ref[r, SPEED_C : SPEED_C + 1, :] = v_ref[0, r : r + 1, :]
        all_ref[r, SPEED_R : SPEED_R + 1, :] = v_ref[1, r : r + 1, :]
    odd = lax.axis_index("row") % 2 == 1
    for k in range(STEPS):
        top, bottom = all_ref[k], all_ref[ROWS - STEPS + k]
        near_ref[k] = jnp.where(odd, top, bottom)
        far_ref[k] = jnp.where(odd, bottom, top)


def packed(strip, place, at):
    total = strip[0:PACK]
    for k in (1, 2):
        part = strip[PACK * k : PACK * (k + 1)] if k == 1 else jnp.concatenate([strip[2 * PACK :], strip[0:8]], 0)
        step = 3 * k if at == 0 else -3 * k
        lo = (at + step) % WIDE
        total = jnp.where((place >= lo) & (place < lo + 3), pltpu.roll(part, step % LANES, 1), total)
    return total


def unpacked(pack, at):
    parts = [pack]
    for k in (1, 2):
        step = -3 * k if at == 0 else 3 * k
        parts.append(pltpu.roll(pack, step % LANES, 1))
    return jnp.concatenate(parts, 0)[0:CHANNELS]


def strip_kernel(all_ref, near_ref, far_ref, token_ref, low_ref, high_ref, left_ref, right_ref, first_ref, second_ref):
    odd = lax.axis_index("row") % 2 == 1
    for k in range(STEPS):
        near, far = near_ref[k], far_ref[k]
        low_ref[k] = jnp.where(odd, near, far)
        high_ref[k] = jnp.where(odd, far, near)
    lane = iota((CHANNELS, LANES), 1)
    left = jnp.broadcast_to(token_ref[0:1, :], (CHANNELS, LANES))
    right = jnp.zeros((CHANNELS, LANES), f32)
    for i in range(ROWS + 6):
        plane = low_ref[i] if i < STEPS else all_ref[i - STEPS] if i < STEPS + ROWS else high_ref[i - STEPS - ROWS]
        at = WIDE * i
        left = jnp.where((lane >= at) & (lane < at + WIDE), pltpu.roll(plane, (at + 3) % LANES, 1), left)
        at = (at - 3) % LANES
        hit = (lane - at) % LANES < WIDE
        right = jnp.where(hit, pltpu.roll(plane, (at + 6) % LANES, 1), right)
    odd = lax.axis_index("col") % 2 == 1
    left_ref[...] = left
    right_ref[...] = right
    place = iota((PACK, LANES), 1)
    left = packed(left, place % WIDE, 0)
    right = packed(right, (place + 3) % LANES % WIDE, 6)
    first_ref[...] = jnp.where(odd, right, left)
    second_ref[...] = jnp.where(odd, left, right)


def prepare_kernel(
    act_ref, w1_ref, w2_ref, w3_ref, b3_ref, pick_ref, w1t_ref, w2t_ref, mix_ref, w3t_ref, bias_ref, token_ref
):
    token_ref[...] = jnp.zeros(token_ref.shape, f32)
    act = act_ref[...].astype(f32)
    before = (iota((LANES, LANES), 0) < iota((LANES, LANES), 1)).astype(f32).astype(bf16)
    inner = jnp.dot(act.astype(bf16), before, preferred_element_type=f32)
    counts = jnp.broadcast_to(jnp.sum(act, axis=1, keepdims=True), (ROWS, LANES))
    row = iota((ROWS, LANES), 0)
    outer = jnp.zeros((ROWS, LANES), f32)
    for k in range(ROWS - 1):
        outer = outer + jnp.where(row > k, jnp.broadcast_to(counts[k : k + 1, :], (ROWS, LANES)), 0.0)
    slot = jnp.where(act > 0.0, inner + outer, -1.0).astype(jnp.int32)
    slots = iota((CAP, LANES), 0)
    for r in range(ROWS):
        hit = slots == jnp.broadcast_to(slot[r : r + 1, :], (CAP, LANES))
        pick_ref[:, r * LANES : (r + 1) * LANES] = jnp.where(hit, 1.0, 0.0).astype(bf16)
    w1t = w1_ref[...].astype(f32)
    w1t_ref[...] = jnp.zeros((2 * CHANNELS, HID), bf16)
    for k in range(2):
        w1t_ref[k * CHANNELS : k * CHANNELS + KINDS + 1, :] = w1t.astype(bf16)
    w2t_ref[...] = w2_ref[...].astype(f32).T.astype(bf16)
    w3t = w3_ref[...].astype(f32).T
    w3t_ref[...] = w3t.astype(bf16)
    part = w1t[0:KINDS, :]
    mix = jnp.dot(w3t.astype(bf16), part.astype(bf16), preferred_element_type=f32)
    mix_ref[...] = (chem_step * mix).astype(bf16)
    shifts = jnp.broadcast_to(b3_ref[...], (KINDS, KINDS))
    same = iota((KINDS, KINDS), 0) == iota((KINDS, KINDS), 1)
    shifts = jnp.sum(jnp.where(same, shifts, 0.0), axis=1, keepdims=True)
    bias_ref[...] = chem_step * jnp.sum(part * shifts, axis=0, keepdims=True)


def face(d_low, d_high, u_low, u_high):
    d = 0.5 * (d_low + d_high)
    u = 0.5 * (u_low + u_high)
    return d - jnp.minimum(u, 0.0), d + jnp.maximum(u, 0.0)


def move_kernel(all_ref, low_ref, high_ref, moved_ref, base_ref, coef_ref, one_ref, two_ref):
    ahead, behind = LANES - 1, 1
    for k in range(4):
        base_ref[k, 0:8, :] = jnp.zeros((8, LANES), f32)
        base_ref[k, 22:32, :] = jnp.zeros((10, LANES), f32)
        for i in range(STEPS):
            base_ref[k, 8 + i : 9 + i, :] = low_ref[i, DIFF + k : DIFF + k + 1, :]
            base_ref[k, 19 + i : 20 + i, :] = high_ref[i, DIFF + k : DIFF + k + 1, :]
        for r in range(ROWS):
            base_ref[k, 11 + r : 12 + r, :] = all_ref[r, DIFF + k : DIFF + k + 1, :]
    d, u, v, inside = (base_ref[k, 8:24, :] for k in range(4))
    a_r, b_r = face(d, pltpu.roll(d, ahead, 1), u, pltpu.roll(u, ahead, 1))
    a_l, b_l = pltpu.roll(a_r, behind, 1), pltpu.roll(b_r, behind, 1)
    a_u, b_u = face(d, base_ref[0, 9:25, :], v, base_ref[2, 9:25, :])
    a_d, b_d = face(base_ref[0, 7:23, :], d, base_ref[2, 7:23, :], v)
    for k, c in enumerate((1.0 - b_r - a_l - b_u - a_d, a_r, b_l, a_u, b_d)):
        coef_ref[k] = inside * c

    def load(step, i):
        if step == 0:
            if i < STEPS:
                return low_ref[i, 0:56, :]
            if i < STEPS + ROWS:
                return all_ref[i - STEPS, 0:56, :]
            return high_ref[i - STEPS - ROWS, 0:56, :]
        return (one_ref if step % 2 else two_ref)[i]

    for step in range(STEPS):
        target = two_ref if step % 2 else one_ref
        for i in range(1 + step, 13 - step):
            mine = load(step, i)
            c = [jnp.broadcast_to(coef_ref[k, i : i + 1, :], (56, LANES)) for k in range(5)]
            new = (
                c[0] * mine
                + c[1] * pltpu.roll(mine, ahead, 1)
                + c[2] * pltpu.roll(mine, behind, 1)
                + c[3] * load(step, i + 1)
                + c[4] * load(step, i - 1)
            )
            if step < STEPS - 1:
                target[i] = new
            else:
                moved_ref[i - STEPS] = new


def move_strip(strip):
    ahead, behind = LANES - 1, 1
    d, u, v, inside = (strip[k : k + 1, :] for k in (DIFF, SPEED_C, SPEED_R, INSIDE))
    a_r, b_r = face(d, pltpu.roll(d, ahead, 1), u, pltpu.roll(u, ahead, 1))
    a_l, b_l = pltpu.roll(a_r, behind, 1), pltpu.roll(b_r, behind, 1)
    a_u, b_u = face(d, pltpu.roll(d, LANES - WIDE, 1), v, pltpu.roll(v, LANES - WIDE, 1))
    a_d, b_d = pltpu.roll(a_u, WIDE, 1), pltpu.roll(b_u, WIDE, 1)
    c = [jnp.broadcast_to(inside * x, (56, LANES)) for x in (1.0 - b_r - a_l - b_u - a_d, a_r, b_l, a_u, b_d)]
    strip = strip[0:56, :]
    for _ in range(STEPS):
        strip = (
            c[0] * strip
            + c[1] * pltpu.roll(strip, ahead, 1)
            + c[2] * pltpu.roll(strip, behind, 1)
            + c[3] * pltpu.roll(strip, LANES - WIDE, 1)
            + c[4] * pltpu.roll(strip, WIDE, 1)
        )
    return strip


def main_kernel(
    moved_ref, left_own, right_own, early_ref, late_ref,
    pick_ref, w1t_ref, w2t_ref, mix_ref, w3t_ref, bias_ref, b1_ref, b2_ref, b3_ref, heat_ref,
    out_ref, full_ref, feat_ref, pre_ref, sum_ref,
):
    lane = iota((CHANNELS, LANES), 1)
    odd = lax.axis_index("col") % 2 == 1
    early, late = early_ref[...], late_ref[...]
    left = jnp.where(lane % WIDE < 3, unpacked(jnp.where(odd, early, late), 0), left_own[...])
    inner = (lane + 3) % LANES % WIDE < 6
    right = jnp.where(inner, right_own[...], unpacked(jnp.where(odd, late, early), 6))
    left, right = move_strip(left), move_strip(right)
    lane = iota((56, LANES), 1)
    place = lane % WIDE
    edges = jnp.where((place >= 3) & (place < 6), left, right)
    outer = (lane < STEPS) | (lane >= LANES - STEPS)
    for r in range(ROWS):
        full_ref[r] = jnp.where(outer, pltpu.roll(edges, (2 * LANES - WIDE * (r + STEPS) - 3) % LANES, 1), moved_ref[r])

    sub = iota((56, LANES), 0)
    for r in range(ROWS):
        block = jnp.where(sub < KINDS, full_ref[r], 0.0)
        block = jnp.where(sub == KINDS, jnp.broadcast_to(heat_ref[r : r + 1, :], (56, LANES)), block)
        block = jnp.concatenate([block, jnp.zeros((8, LANES), f32)], 0)
        coarse = block.astype(bf16)
        fine = jnp.where(iota((CHANNELS, LANES), 0) < KINDS, block - coarse.astype(f32), 0.0).astype(bf16)
        feat_ref[0:CHANNELS, r * LANES : (r + 1) * LANES] = coarse
        feat_ref[CHANNELS:, r * LANES : (r + 1) * LANES] = fine
    slots = lax.dot_general(pick_ref[...], feat_ref[...], (((1,), (1,)), ((), ())), preferred_element_type=f32)
    for k in range(CAP // CHUNK):
        s = slice(k * CHUNK, (k + 1) * CHUNK)
        pre_ref[s, :] = jnp.dot(slots[s, :].astype(bf16), w1t_ref[...], preferred_element_type=f32) + b1_ref[...]
    parts = [slice(k * CHUNK, (k + 1) * CHUNK) for k in range(CAP // CHUNK)]
    for index in range(SUBSTEPS):
        first = [jnp.tanh(pre_ref[s, :]).astype(bf16) for s in parts]
        second = [jnp.dot(h, w2t_ref[...], preferred_element_type=f32) + b2_ref[...] for h in first]
        second = [jnp.tanh(h).astype(bf16) for h in second]
        for s, h in zip(parts, second):
            wide = h.astype(f32)
            sum_ref[s, :] = wide if index == 0 else sum_ref[s, :] + wide
            if index < SUBSTEPS - 1:
                pre_ref[s, :] += jnp.dot(h, mix_ref[...], preferred_element_type=f32) + bias_ref[...]
    total = sum_ref[...]
    high = total.astype(bf16)
    low = (total - high.astype(f32)).astype(bf16)
    rate = jnp.dot(high, w3t_ref[...], preferred_element_type=f32) + jnp.dot(low, w3t_ref[...], preferred_element_type=f32)
    rate = chem_step * (rate + SUBSTEPS * b3_ref[...])
    rate = jnp.concatenate([rate, jnp.zeros((CAP, LANES - KINDS), f32)], 1).T[0:CHANNELS, :]
    high = rate.astype(bf16)
    low = (rate - high.astype(f32)).astype(bf16)
    both = jnp.concatenate([high, low], 0)
    for r in range(0, ROWS, 2):
        gain = jnp.dot(both, pick_ref[:, r * LANES : (r + 2) * LANES], preferred_element_type=f32)
        gain = gain[0:CHANNELS] + gain[CHANNELS:]
        for k in range(2):
            block = full_ref[r + k] + gain[0:56, k * LANES : (k + 1) * LANES]
            out_ref[pl.ds(r + k, KINDS, stride=ROWS), :] = block[0:KINDS]


def stay(x):
    return pltpu.with_memory_space_constraint(x, pltpu.HBM)


def call(kernel, shapes, operands, scratch=(), copies=0, cost=None):
    return pl.pallas_call(
        kernel,
        out_shape=[jax.ShapeDtypeStruct(s, t) for s, t in shapes],
        in_specs=[pl.BlockSpec(memory_space=pltpu.HBM if copies else pltpu.VMEM)] * len(operands),
        out_specs=[pl.BlockSpec(memory_space=pltpu.VMEM)] * len(shapes),
        scratch_shapes=[pltpu.VMEM(s, t) for s, t in scratch] + [pltpu.SemaphoreType.DMA((copies,))] * (copies > 0),
        compiler_params=pltpu.CompilerParams(vmem_limit_bytes=16 << 20),
        cost_estimate=cost and pl.CostEstimate(flops=cost, bytes_accessed=0, transcendentals=0),
    )(*operands)


def swaps(devices, first):
    low = range(first, devices - 1, 2)
    return [(i, i + 1) for i in low] + [(i + 1, i) for i in low]


def shards(y, d, v, heat, active, w1, b1, w2, b2, w3, b3):
    plane = (CHANNELS, LANES)
    edge = ((STEPS,) + plane, f32)
    tile = (ROWS, LANES)
    every, near, far, active, heat, b1, b2, b3 = call(
        planes_kernel,
        [
            ((ROWS,) + plane, f32), edge, edge, (tile, jnp.int32), (tile, f32),
            ((1, HID), f32), ((1, HID), f32), ((1, KINDS), f32),
        ],
        [stay(x) for x in (y.reshape(KINDS * ROWS, LANES), d, v, active, heat, b1[None], b2[None], b3[None])],
        scratch=[((KINDS * ROWS, LANES), f32), (tile, f32), ((2,) + tile, f32)], copies=8,
    )
    devices = lax.axis_size("row")
    far = lax.ppermute(far, "row", swaps(devices, 1))
    near = lax.ppermute(near, "row", swaps(devices, 0))
    *picks, token = call(
        prepare_kernel,
        [
            ((CAP, ROWS * LANES), bf16), ((2 * CHANNELS, HID), bf16), ((HID, HID), bf16), ((HID, HID), bf16),
            ((HID, KINDS), bf16), ((1, HID), f32), (tile, f32),
        ],
        (active, w1.T, w2, w3, b3),
        cost=COST_PREPARE,
    )
    pack = ((PACK, LANES), f32)
    low, high, left_own, right_own, first, second = call(
        strip_kernel, [edge, edge, (plane, f32), (plane, f32), pack, pack], (every, near, far, token)
    )
    devices = lax.axis_size("col")
    early = lax.ppermute(first, "col", swaps(devices, 0))
    late = lax.ppermute(second, "col", swaps(devices, 1))
    (moved,) = call(
        move_kernel, [((ROWS, 56, LANES), f32)], (every, low, high),
        scratch=[((4, 32, LANES), f32), ((5, 16, LANES), f32), ((14, 56, LANES), f32), ((14, 56, LANES), f32)],
        cost=COST_MOVE,
    )
    (out,) = call(
        main_kernel,
        [((KINDS * ROWS, LANES), f32)],
        (moved, left_own, right_own, early, late, *picks, b1, b2, b3, heat),
        scratch=[
            ((ROWS, 56, LANES), f32), ((2 * CHANNELS, ROWS * LANES), bf16), ((CAP, HID), f32), ((CAP, HID), f32),
        ],
    )
    return out.reshape(KINDS, ROWS, LANES)


def solution(mesh):
    tile, rest = P("row", "col"), P()
    stack = P(None, "row", "col")
    in_specs = (stack, tile, stack, tile, tile, rest, rest, rest, rest, rest, rest)
    return jax.shard_map(shards, mesh=mesh, in_specs=in_specs, out_specs=stack, check_vma=False)
```

```python
import jax
import jax.numpy as jnp
from jax import lax
from jax.experimental import pallas as pl
from jax.experimental.pallas import tpu as pltpu
from jax.sharding import PartitionSpec as P


SUBSTEPS = 8
STEPS = 3
KINDS = 54
HID = 256
ROWS = 8
LANES = 128
CAP = 384
CHUNK = 192
CHANNELS = 64
DIFF, SPEED_C, SPEED_R, INSIDE = 54, 55, 56, 57
WIDE = 9
COST_PREPARE = 20_000_000
COST_MOVE = 20_000_000
chem_step = 0.0625
f32 = jnp.float32
bf16 = jnp.bfloat16


def iota(shape, axis):
    return lax.broadcasted_iota(jnp.int32, shape, axis)


def planes_kernel(
    y_hbm, d_hbm, v_hbm, act_hbm, heat_hbm, b1_hbm, b2_hbm, b3_hbm,
    all_ref, near_ref, far_ref, act_ref, heat_ref, b1_ref, b2_ref, b3_ref, y_ref, d_ref, v_ref, sems,
):
    pairs = (
        (y_hbm, y_ref), (d_hbm, d_ref), (v_hbm, v_ref), (act_hbm, act_ref), (heat_hbm, heat_ref),
        (b1_hbm, b1_ref), (b2_hbm, b2_ref), (b3_hbm, b3_ref),
    )
    copies = [pltpu.make_async_copy(source, target, sems.at[k]) for k, (source, target) in enumerate(pairs)]
    for copy in copies:
        copy.start()
    for r in range(ROWS):
        all_ref[r, INSIDE:CHANNELS, :] = jnp.ones((CHANNELS - INSIDE, LANES), f32)
    for copy in copies:
        copy.wait()
    for r in range(ROWS):
        all_ref[r, 0:KINDS, :] = y_ref[pl.ds(r, KINDS, stride=ROWS), :]
        all_ref[r, DIFF : DIFF + 1, :] = d_ref[r : r + 1, :]
        all_ref[r, SPEED_C : SPEED_C + 1, :] = v_ref[0, r : r + 1, :]
        all_ref[r, SPEED_R : SPEED_R + 1, :] = v_ref[1, r : r + 1, :]
    odd = lax.axis_index("row") % 2 == 1
    for k in range(STEPS):
        top, bottom = all_ref[k], all_ref[ROWS - STEPS + k]
        near_ref[k] = jnp.where(odd, top, bottom)
        far_ref[k] = jnp.where(odd, bottom, top)


def strip_kernel(all_ref, near_ref, far_ref, token_ref, low_ref, high_ref, first_ref, second_ref):
    odd = lax.axis_index("row") % 2 == 1
    for k in range(STEPS):
        near, far = near_ref[k], far_ref[k]
        low_ref[k] = jnp.where(odd, near, far)
        high_ref[k] = jnp.where(odd, far, near)
    lane = iota((CHANNELS, LANES), 1)
    left = jnp.broadcast_to(token_ref[0:1, :], (CHANNELS, LANES))
    right = jnp.zeros((CHANNELS, LANES), f32)
    for i in range(ROWS + 6):
        plane = low_ref[i] if i < STEPS else all_ref[i - STEPS] if i < STEPS + ROWS else high_ref[i - STEPS - ROWS]
        at = WIDE * i
        left = jnp.where((lane >= at) & (lane < at + WIDE), pltpu.roll(plane, (at + 3) % LANES, 1), left)
        at = (at - 3) % LANES
        hit = (lane - at) % LANES < WIDE
        right = jnp.where(hit, pltpu.roll(plane, (at + 6) % LANES, 1), right)
    odd = lax.axis_index("col") % 2 == 1
    first_ref[...] = jnp.where(odd, right, left)
    second_ref[...] = jnp.where(odd, left, right)


def prepare_kernel(
    act_ref, w1_ref, w2_ref, w3_ref, b3_ref, pick_ref, w1t_ref, w2t_ref, mix_ref, w3p_ref, bias_ref, shift_ref, token_ref
):
    token_ref[...] = jnp.zeros(token_ref.shape, f32)
    act = act_ref[...].astype(f32)
    before = (iota((LANES, LANES), 0) < iota((LANES, LANES), 1)).astype(f32).astype(bf16)
    inner = jnp.dot(act.astype(bf16), before, preferred_element_type=f32)
    counts = jnp.broadcast_to(jnp.sum(act, axis=1, keepdims=True), (ROWS, LANES))
    row = iota((ROWS, LANES), 0)
    outer = jnp.zeros((ROWS, LANES), f32)
    for k in range(ROWS - 1):
        outer = outer + jnp.where(row > k, jnp.broadcast_to(counts[k : k + 1, :], (ROWS, LANES)), 0.0)
    slot = jnp.where(act > 0.0, inner + outer, -1.0).astype(jnp.int32)
    slots = iota((CAP, LANES), 0)
    for r in range(ROWS):
        hit = slots == jnp.broadcast_to(slot[r : r + 1, :], (CAP, LANES))
        pick_ref[:, r * LANES : (r + 1) * LANES] = jnp.where(hit, 1.0, 0.0).astype(bf16)
    w1t = w1_ref[...].astype(f32)
    w1t_ref[...] = jnp.zeros((2 * CHANNELS, HID), bf16)
    for k in range(2):
        w1t_ref[k * CHANNELS : k * CHANNELS + KINDS + 1, :] = w1t.astype(bf16)
    w2t_ref[...] = w2_ref[...].astype(f32).T.astype(bf16)
    w3t = w3_ref[...].astype(f32).T
    w3p_ref[...] = jnp.zeros((CHANNELS, HID), bf16)
    w3p_ref[0:KINDS, :] = w3_ref[...]
    part = w1t[0:KINDS, :]
    mix = jnp.dot(w3t.astype(bf16), part.astype(bf16), preferred_element_type=f32)
    mix_ref[...] = (chem_step * mix).astype(bf16)
    shifts = jnp.broadcast_to(b3_ref[...], (KINDS, KINDS))
    same = iota((KINDS, KINDS), 0) == iota((KINDS, KINDS), 1)
    shifts = jnp.sum(jnp.where(same, shifts, 0.0), axis=1, keepdims=True)
    bias_ref[...] = chem_step * jnp.sum(part * shifts, axis=0, keepdims=True)
    shift_ref[...] = jnp.zeros((CHANNELS, LANES), f32)
    shift_ref[0:KINDS, :] = jnp.broadcast_to(SUBSTEPS * shifts, (KINDS, LANES))


def face(d_low, d_high, u_low, u_high):
    d = 0.5 * (d_low + d_high)
    u = 0.5 * (u_low + u_high)
    return d - jnp.minimum(u, 0.0), d + jnp.maximum(u, 0.0)


def move_kernel(all_ref, low_ref, high_ref, moved_ref, base_ref, coef_ref, one_ref, two_ref):
    ahead, behind = LANES - 1, 1
    for k in range(4):
        base_ref[k, 0:8, :] = jnp.zeros((8, LANES), f32)
        base_ref[k, 22:32, :] = jnp.zeros((10, LANES), f32)
        for i in range(STEPS):
            base_ref[k, 8 + i : 9 + i, :] = low_ref[i, DIFF + k : DIFF + k + 1, :]
            base_ref[k, 19 + i : 20 + i, :] = high_ref[i, DIFF + k : DIFF + k + 1, :]
        for r in range(ROWS):
            base_ref[k, 11 + r : 12 + r, :] = all_ref[r, DIFF + k : DIFF + k + 1, :]
    d, u, v, inside = (base_ref[k, 8:24, :] for k in range(4))
    a_r, b_r = face(d, pltpu.roll(d, ahead, 1), u, pltpu.roll(u, ahead, 1))
    a_l, b_l = pltpu.roll(a_r, behind, 1), pltpu.roll(b_r, behind, 1)
    a_u, b_u = face(d, base_ref[0, 9:25, :], v, base_ref[2, 9:25, :])
    a_d, b_d = face(base_ref[0, 7:23, :], d, base_ref[2, 7:23, :], v)
    for k, c in enumerate((1.0 - b_r - a_l - b_u - a_d, a_r, b_l, a_u, b_d)):
        coef_ref[k] = inside * c

    def load(step, i):
        if step == 0:
            if i < STEPS:
                return low_ref[i, 0:56, :]
            if i < STEPS + ROWS:
                return all_ref[i - STEPS, 0:56, :]
            return high_ref[i - STEPS - ROWS, 0:56, :]
        return (one_ref if step % 2 else two_ref)[i]

    for step in range(STEPS):
        target = two_ref if step % 2 else one_ref
        for i in range(1 + step, 13 - step):
            mine = load(step, i)
            c = [jnp.broadcast_to(coef_ref[k, i : i + 1, :], (56, LANES)) for k in range(5)]
            new = (
                c[0] * mine
                + c[1] * pltpu.roll(mine, ahead, 1)
                + c[2] * pltpu.roll(mine, behind, 1)
                + c[3] * load(step, i + 1)
                + c[4] * load(step, i - 1)
            )
            if step < STEPS - 1:
                target[i] = new
            else:
                moved_ref[i - STEPS] = new


def move_strip(strip):
    ahead, behind = LANES - 1, 1
    d, u, v, inside = (strip[k : k + 1, :] for k in (DIFF, SPEED_C, SPEED_R, INSIDE))
    a_r, b_r = face(d, pltpu.roll(d, ahead, 1), u, pltpu.roll(u, ahead, 1))
    a_l, b_l = pltpu.roll(a_r, behind, 1), pltpu.roll(b_r, behind, 1)
    a_u, b_u = face(d, pltpu.roll(d, LANES - WIDE, 1), v, pltpu.roll(v, LANES - WIDE, 1))
    a_d, b_d = pltpu.roll(a_u, WIDE, 1), pltpu.roll(b_u, WIDE, 1)
    c = [jnp.broadcast_to(inside * x, (56, LANES)) for x in (1.0 - b_r - a_l - b_u - a_d, a_r, b_l, a_u, b_d)]
    strip = strip[0:56, :]
    for _ in range(STEPS):
        strip = (
            c[0] * strip
            + c[1] * pltpu.roll(strip, ahead, 1)
            + c[2] * pltpu.roll(strip, behind, 1)
            + c[3] * pltpu.roll(strip, LANES - WIDE, 1)
            + c[4] * pltpu.roll(strip, WIDE, 1)
        )
    return strip


def main_kernel(
    moved_ref, first_ref, second_ref, early_ref, late_ref,
    pick_ref, w1t_ref, w2t_ref, mix_ref, w3p_ref, bias_ref, shift_ref, b1_ref, b2_ref, heat_ref,
    out_ref, full_ref, feat_ref, pre_ref, sum_ref,
):
    lane = iota((CHANNELS, LANES), 1)
    odd = lax.axis_index("col") % 2 == 1
    first, second, early, late = first_ref[...], second_ref[...], early_ref[...], late_ref[...]
    left = jnp.where(lane % WIDE < 3, jnp.where(odd, early, late), jnp.where(odd, second, first))
    inner = (lane + 3) % LANES % WIDE < 6
    right = jnp.where(inner, jnp.where(odd, first, second), jnp.where(odd, late, early))
    left, right = move_strip(left), move_strip(right)
    lane = iota((56, LANES), 1)
    place = lane % WIDE
    edges = jnp.where((place >= 3) & (place < 6), left, right)
    outer = (lane < STEPS) | (lane >= LANES - STEPS)
    for r in range(ROWS):
        full_ref[r] = jnp.where(outer, pltpu.roll(edges, (2 * LANES - WIDE * (r + STEPS) - 3) % LANES, 1), moved_ref[r])

    sub = iota((56, LANES), 0)
    for r in range(ROWS):
        block = jnp.where(sub < KINDS, full_ref[r], 0.0)
        block = jnp.where(sub == KINDS, jnp.broadcast_to(heat_ref[r : r + 1, :], (56, LANES)), block)
        block = jnp.concatenate([block, jnp.zeros((8, LANES), f32)], 0)
        coarse = block.astype(bf16)
        fine = jnp.where(iota((CHANNELS, LANES), 0) < KINDS, block - coarse.astype(f32), 0.0).astype(bf16)
        feat_ref[0:CHANNELS, r * LANES : (r + 1) * LANES] = coarse
        feat_ref[CHANNELS:, r * LANES : (r + 1) * LANES] = fine
    slots = lax.dot_general(pick_ref[...], feat_ref[...], (((1,), (1,)), ((), ())), preferred_element_type=f32)
    for k in range(CAP // CHUNK):
        s = slice(k * CHUNK, (k + 1) * CHUNK)
        pre_ref[s, :] = jnp.dot(slots[s, :].astype(bf16), w1t_ref[...], preferred_element_type=f32) + b1_ref[...]
    parts = [slice(k * CHUNK, (k + 1) * CHUNK) for k in range(CAP // CHUNK)]
    for index in range(SUBSTEPS):
        first = [jnp.tanh(pre_ref[s, :]).astype(bf16) for s in parts]
        second = [jnp.dot(h, w2t_ref[...], preferred_element_type=f32) + b2_ref[...] for h in first]
        second = [jnp.tanh(h).astype(bf16) for h in second]
        for s, h in zip(parts, second):
            wide = h.astype(f32)
            sum_ref[s, :] = wide if index == 0 else sum_ref[s, :] + wide
            if index < SUBSTEPS - 1:
                pre_ref[s, :] += jnp.dot(h, mix_ref[...], preferred_element_type=f32) + bias_ref[...]
    total = sum_ref[...]
    high = total.astype(bf16)
    low = (total - high.astype(f32)).astype(bf16)
    turned = lambda x: lax.dot_general(w3p_ref[...], x, (((1,), (1,)), ((), ())), preferred_element_type=f32)
    rate = turned(high) + turned(low)
    rate = chem_step * (rate + jnp.concatenate([shift_ref[...]] * (CAP // LANES), 1))
    high = rate.astype(bf16)
    low = (rate - high.astype(f32)).astype(bf16)
    both = jnp.concatenate([high, low], 0)
    for r in range(0, ROWS, 2):
        gain = jnp.dot(both, pick_ref[:, r * LANES : (r + 2) * LANES], preferred_element_type=f32)
        gain = gain[0:CHANNELS] + gain[CHANNELS:]
        for k in range(2):
            block = full_ref[r + k] + gain[0:56, k * LANES : (k + 1) * LANES]
            out_ref[pl.ds(r + k, KINDS, stride=ROWS), :] = block[0:KINDS]


def stay(x):
    return pltpu.with_memory_space_constraint(x, pltpu.HBM)


def call(kernel, shapes, operands, scratch=(), copies=0, cost=None):
    return pl.pallas_call(
        kernel,
        out_shape=[jax.ShapeDtypeStruct(s, t) for s, t in shapes],
        in_specs=[pl.BlockSpec(memory_space=pltpu.HBM if copies else pltpu.VMEM)] * len(operands),
        out_specs=[pl.BlockSpec(memory_space=pltpu.VMEM)] * len(shapes),
        scratch_shapes=[pltpu.VMEM(s, t) for s, t in scratch] + [pltpu.SemaphoreType.DMA((copies,))] * (copies > 0),
        compiler_params=pltpu.CompilerParams(vmem_limit_bytes=16 << 20),
        cost_estimate=cost and pl.CostEstimate(flops=cost, bytes_accessed=0, transcendentals=0),
    )(*operands)


def swaps(devices, first):
    low = range(first, devices - 1, 2)
    return [(i, i + 1) for i in low] + [(i + 1, i) for i in low]


def shards(y, d, v, heat, active, w1, b1, w2, b2, w3, b3):
    plane = (CHANNELS, LANES)
    edge = ((STEPS,) + plane, f32)
    tile = (ROWS, LANES)
    every, near, far, active, heat, b1, b2, b3 = call(
        planes_kernel,
        [
            ((ROWS,) + plane, f32), edge, edge, (tile, jnp.int32), (tile, f32),
            ((1, HID), f32), ((1, HID), f32), ((1, KINDS), f32),
        ],
        [stay(x) for x in (y.reshape(KINDS * ROWS, LANES), d, v, active, heat, b1[None], b2[None], b3[None])],
        scratch=[((KINDS * ROWS, LANES), f32), (tile, f32), ((2,) + tile, f32)], copies=8,
    )
    devices = lax.axis_size("row")
    far = lax.ppermute(far, "row", swaps(devices, 1))
    near = lax.ppermute(near, "row", swaps(devices, 0))
    *picks, token = call(
        prepare_kernel,
        [
            ((CAP, ROWS * LANES), bf16), ((2 * CHANNELS, HID), bf16), ((HID, HID), bf16), ((HID, HID), bf16),
            ((CHANNELS, HID), bf16), ((1, HID), f32), (plane, f32), (tile, f32),
        ],
        (active, w1.T, w2, w3, b3),
        cost=COST_PREPARE,
    )
    low, high, first, second = call(strip_kernel, [edge, edge, (plane, f32), (plane, f32)], (every, near, far, token))
    devices = lax.axis_size("col")
    early = lax.ppermute(first, "col", swaps(devices, 0))
    late = lax.ppermute(second, "col", swaps(devices, 1))
    (moved,) = call(
        move_kernel, [((ROWS, 56, LANES), f32)], (every, low, high),
        scratch=[((4, 32, LANES), f32), ((5, 16, LANES), f32), ((14, 56, LANES), f32), ((14, 56, LANES), f32)],
        cost=COST_MOVE,
    )
    (out,) = call(
        main_kernel,
        [((KINDS * ROWS, LANES), f32)],
        (moved, first, second, early, late, *picks, b1, b2, heat),
        scratch=[
            ((ROWS, 56, LANES), f32), ((2 * CHANNELS, ROWS * LANES), bf16), ((CAP, HID), f32), ((CAP, HID), f32),
        ],
    )
    return out.reshape(KINDS, ROWS, LANES)


def solution(mesh):
    tile, rest = P("row", "col"), P()
    stack = P(None, "row", "col")
    in_specs = (stack, tile, stack, tile, tile, rest, rest, rest, rest, rest, rest)
    return jax.shard_map(shards, mesh=mesh, in_specs=in_specs, out_specs=stack, check_vma=False)
```
